32 devices in a mesh: tok: 8 (over z, y), voc: 4 (over x, core).
Axes of the slice: x: 2, y: 2, z: 4, core: 2. Of those that a mesh axis runs over, the one named last changes fastest.
Arguments:
- teacher_logits: bfloat16 [1024, 76032], P('tok', 'voc'), may hold values from -1000 to 1000
- student_logits: bfloat16 [1024, 76032], P('tok', 'voc'), may hold values from -1000 to 1000
- target_ids: int32 [1024], P('tok'), may hold values from -1 to 76031, as said below
- vocab_used: int32 [76032], replicated, may hold values from 0 to 1
Outputs:
- logit_grad: bfloat16 [1024, 76032], P('tok', 'voc')
- token_loss: float32 [1024], P('tok')
The draws below stay inside these ranges and needn't reach their ends.
Inputs may be any that keep to these rules, and one draw needn't show every extreme that they name: `target_ids`: every entry that is not -1 names a vocabulary entry v with vocab_used[v] == 1; the first token of every 128 is never -1.
All inputs are finite; a program needn't handle non-finite values.
Results may differ from the reference program's by a relative error of at most 0.0004.
Values may be sent and summed in bfloat16 or wider, within the bound.
No kernel may reach another device: no remote copies, remote signals or barrier semaphores. Data moves between devices by JAX's collectives and lax.ppermute only.
A program may use at most 64 MiB of HBM per device.

```python
import jax
import jax.numpy as jnp
from jax import lax

VOCAB = 76032
TOK_DEV = 128
TOKENS = 1024
BLOCK = 4752
N_VOC = 4


def logit_field(key, height, breadth):
    keys = jax.random.split(key, 1)
    base = jnp.clip(jax.random.normal(keys[0], (height, breadth), jnp.float32), -8.0, 8.0)
    return 3.0 * base


def token_draw(key):
    base_key = jax.random.fold_in(key, 5)
    keys = jax.random.split(base_key, 3)
    candidate = jax.random.randint(keys[0], (TOKENS,), 0, VOCAB)
    candidate = candidate.at[0].set(VOCAB - 1)
    roll = jax.random.randint(keys[1], (TOKENS,), 0, 4 * TOKENS)
    position = jnp.arange(TOKENS)
    kept = (roll < TOKENS + 2 * position) | (position % TOK_DEV == 0)
    targets = jnp.where(kept, candidate, -1).astype(jnp.int32)
    used_flags = (jax.random.randint(keys[2], (VOCAB,), 0, 16) != 0).astype(jnp.int32)
    used_flags = used_flags.at[candidate].set(1)
    return (targets, used_flags)


def draw_teacher_logits(key, part):
    return logit_field(jax.random.fold_in(key, 11), TOKENS, VOCAB).astype(jnp.bfloat16)


def draw_student_logits(key, part):
    return logit_field(jax.random.fold_in(key, 12), TOKENS, VOCAB).astype(jnp.bfloat16)


def draw_target_ids(key, part):
    return token_draw(key)[0]


def draw_vocab_used(key, part):
    return token_draw(key)[1]


def setup_inputs(seed: int = 0) -> dict:
    splits = jax.random.split(jax.random.key(seed), 5)
    teacher_logits = draw_teacher_logits(jax.random.fold_in(splits[4], 71), 0)
    student_logits = draw_student_logits(jax.random.fold_in(splits[4], 71), 0)
    target_ids = draw_target_ids(jax.random.fold_in(splits[4], 71), 0)
    vocab_used = draw_vocab_used(jax.random.fold_in(splits[4], 71), 0)
    return {"teacher_logits": teacher_logits, "student_logits": student_logits, "target_ids": target_ids, "vocab_used": vocab_used}


SENTINEL = -1e30


def reorder_columns(matrix):
    height = matrix.shape[0]
    split = matrix.reshape(height, N_VOC, N_VOC, BLOCK)
    return split.transpose(0, 2, 1, 3).reshape(height, VOCAB)


def log_total(values, used):
    masked = jnp.where(used, values, SENTINEL)
    top_value = jnp.max(masked, axis=1)
    total = jnp.sum(jnp.where(used, jnp.exp(values - top_value[:, None]), 0.0), axis=1)
    return top_value + jnp.log(total)


def reference(teacher_logits, student_logits, target_ids, vocab_used):
    used = (vocab_used == 1)[None, :]
    kept = target_ids >= 0
    kept_count = jnp.sum(kept.astype(jnp.float32))
    hard_weight = jnp.where(kept, 0.5 * TOKENS / kept_count, 0.0).astype(jnp.float32)
    blocks_count = TOKENS // TOK_DEV
    columns = jnp.arange(VOCAB, dtype=jnp.int32)

    def one_block(pieces):
        teacher_blk, student_blk, target_blk, weight_blk = pieces
        teacher = teacher_blk.astype(jnp.float32)
        student = reorder_columns(student_blk).astype(jnp.float32)
        teacher_lse = log_total(teacher, used)
        student_lse = log_total(student, used)
        teacher_prob = jnp.where(used, jnp.exp(teacher - teacher_lse[:, None]), 0.0)
        student_prob = jnp.where(used, jnp.exp(student - student_lse[:, None]), 0.0)
        divergence = jnp.sum(teacher_prob * (teacher - student), axis=1) - teacher_lse + student_lse
        onehot = columns[None, :] == target_blk[:, None]
        target_logit = jnp.sum(jnp.where(onehot, student, 0.0), axis=1)
        loss_blk = 0.5 * divergence + weight_blk * (student_lse - target_logit)
        grad = 0.5 * (student_prob - teacher_prob) + weight_blk[:, None] * (student_prob - onehot.astype(jnp.float32))
        grad = jnp.where(used, grad, 0.0).astype(jnp.bfloat16)
        return reorder_columns(grad), loss_blk

    grads, losses = lax.map(one_block, (
        teacher_logits.reshape(blocks_count, TOK_DEV, VOCAB),
        student_logits.reshape(blocks_count, TOK_DEV, VOCAB),
        target_ids.reshape(blocks_count, TOK_DEV),
        hard_weight.reshape(blocks_count, TOK_DEV)))
    return grads.reshape(TOKENS, VOCAB), losses.reshape(TOKENS)
```

```python
import functools

import jax
import jax.numpy as jnp
import numpy as np
from jax import lax
from jax.experimental import pallas as pl
from jax.experimental.pallas import tpu as pltpu
from jax.sharding import PartitionSpec as P

NEG = -1e30
LOW = -3e38
ROWS = 16
LINES = 8
LN2 = 0.6931471805599453
F32 = jnp.float32
BF16 = jnp.bfloat16


def largest_part(total, limit):
    best = ROWS
    for size in range(ROWS, limit + 1, ROWS):
        if total % size == 0:
            best = size
    return best


def fold(op, value, height=8):
    return op(value.reshape(-1, height, value.shape[-1]), axis=0)


def mask_bias(mask_ref, n):
    lines = mask_ref[n]
    ones = jnp.ones((lines.shape[0], 128), BF16)
    spread = lax.dot_general(lines, ones, (((0,), (0,)), ((), ())), preferred_element_type=F32)
    return spread.astype(BF16)


def wide_rows(line, height):
    return jnp.broadcast_to(line, (height, line.shape[-1]))


def stats_kernel(t_ref, tb_ref, s_ref, sb_ref, *rest, step, counts):
    ids, (o_ref, mt, ms, lt, ls, t_held, s_held) = rest[:-7], rest[-7:]
    g = pl.program_id(0)
    rows, lanes = t_ref.shape

    @pl.when(g == 0)
    def _():
        mt[...] = jnp.full(mt.shape, LOW, F32)
        ms[...] = jnp.full(ms.shape, LOW, F32)
        lt[...] = jnp.zeros(lt.shape, F32)
        ls[...] = jnp.zeros(ls.shape, F32)

    def part(n):
        return pl.ds(pl.multiple_of(n * step, step), step)

    def first(n, carry):
        t = t_ref[part(n), :] + mask_bias(tb_ref, n)
        s = s_ref[part(n), :] + mask_bias(sb_ref, n)
        t_held[part(n), :] = t
        s_held[part(n), :] = s
        return (
            jnp.maximum(carry[0], fold(jnp.max, t, 16)),
            jnp.maximum(carry[1], fold(jnp.max, s, 16)),
        )

    low = jnp.full((16, lanes), LOW, BF16)
    t_high, s_high = lax.fori_loop(0, rows // step, first, (low, low))
    a = jnp.maximum(mt[...], fold(jnp.max, t_high.astype(F32)))
    b = jnp.maximum(ms[...], fold(jnp.max, s_high.astype(F32)))

    def spread(top):
        return jnp.broadcast_to(top[None], (step // 8, 8, lanes)).reshape(step, lanes)

    def second(n, carry):
        return (
            carry[0] + fold(jnp.sum, jnp.exp(t_held[part(n), :].astype(F32) - spread(a))),
            carry[1] + fold(jnp.sum, jnp.exp(s_held[part(n), :].astype(F32) - spread(b))),
        )

    start = (lt[...] * jnp.exp(mt[...] - a), ls[...] * jnp.exp(ms[...] - b))
    p, q = lax.fori_loop(0, rows // step, second, start)
    mt[...] = a
    ms[...] = b
    lt[...] = p
    ls[...] = q

    @pl.when(g == pl.num_programs(0) - 1)
    def _():
        def close(m, l):
            top = jnp.max(m, axis=0, keepdims=True)
            return top, jnp.sum(l * jnp.exp(m - top), axis=0, keepdims=True)

        t_top, t_sum = close(a, p)
        s_top, s_sum = close(b, q)
        kept = jnp.zeros((1, lanes), F32)
        for ref, counted in zip(ids, counts):
            share = jnp.where(ref[...] >= 0, 1.0, 0.0)
            if counted is not None:
                share = jnp.where(lax.axis_index("voc") < counted, share, 0.0)
            kept = kept + share
        o_ref[...] = jnp.concatenate(
            [t_top, t_sum, s_top, s_sum, kept, jnp.zeros((3, lanes), F32)], axis=0)


def run_stats(teacher, student, bias, ids, counts, limit):
    total, lanes = teacher.shape
    rows = largest_part(total, limit)
    count = total // rows
    near = pl.BlockSpec((rows, lanes), lambda g: (g, 0))
    step = bias.shape[-1]
    lines = (rows // step,) + bias.shape[1:]
    t_mask = pl.BlockSpec(lines, lambda g: (g, 0, 0))
    s_mask = pl.BlockSpec(lines, lambda g: (g + count, 0, 0))
    one = pl.BlockSpec((1, lanes), lambda g: (0, 0))

    def kernel(*refs):
        stats_kernel(*refs, step=step, counts=counts)

    return pl.pallas_call(
        kernel,
        out_shape=jax.ShapeDtypeStruct((8, lanes), F32),
        grid=(count,),
        in_specs=[near, t_mask, near, s_mask] + [one] * len(ids),
        out_specs=pl.BlockSpec((8, lanes), lambda g: (0, 0)),
        scratch_shapes=[pltpu.VMEM((8, lanes), F32)] * 4 + [pltpu.VMEM((rows, lanes), BF16)] * 2,
        compiler_params=pltpu.CompilerParams(dimension_semantics=("arbitrary",)),
        name="stats",
    )(teacher, bias, student, bias, *ids)


def join_stats(refs, target, tokens):
    parts = [ref[...] for ref in refs]
    t_top = parts[0][0:1]
    s_top = parts[0][2:3]
    kept = parts[0][4:5]
    for part in parts[1:]:
        t_top = jnp.maximum(t_top, part[0:1])
        s_top = jnp.maximum(s_top, part[2:3])
        kept = kept + part[4:5]
    t_sum = jnp.zeros_like(t_top)
    s_sum = jnp.zeros_like(t_top)
    for part in parts:
        t_sum = t_sum + part[1:2] * jnp.exp(part[0:1] - t_top)
        s_sum = s_sum + part[3:4] * jnp.exp(part[2:3] - s_top)
    t_lse = t_top + jnp.log(t_sum)
    s_lse = s_top + jnp.log(s_sum)
    count = jnp.sum(kept, axis=1, keepdims=True)
    weight = jnp.where(target >= 0, (0.5 * tokens) / count, 0.0)
    base = (0.5 * (s_lse - t_lse) + weight * s_lse) * (1.0 / len(parts))
    blank = jnp.zeros((4, target.shape[1]), F32)
    return jnp.concatenate([t_lse + LN2, s_lse - jnp.log(0.5 + weight), weight, base, blank], axis=0)


def chunk_kernel(spots, *refs, spans, slot, step, cols, shares, tokens, last):
    pieces, refs = refs[:len(spans)], refs[len(spans):]
    s_ref, b_ref, tgt_ref = refs[:3]
    refs = refs[3:]
    g = pl.program_id(0)
    rows, lanes = s_ref.shape
    if shares:
        share_refs, (g_ref, d_out, vec_ref) = refs[:shares], refs[shares:]

        @pl.when(g == 0)
        def _():
            vec_ref[...] = join_stats(share_refs, tgt_ref[...], tokens)
            d_out[...] = jnp.zeros(d_out.shape, F32)
    else:
        vec_ref, d_in, _, g_ref, d_out = refs[:5]
        if last:
            d_sum = refs[5]
        else:
            d_sum = d_out

            @pl.when(g == 0)
            def _():
                d_out[...] = d_in[...]
    if shares:
        d_sum = d_out
    if last:
        @pl.when(g == 0)
        def _():
            d_sum[...] = d_in[...]

    at = 3 * (slot + g)
    base = spots[at + 1]
    target = wide_rows(tgt_ref[...], 8)
    iota = lax.broadcasted_iota(jnp.int32, (step, lanes), 0)
    t_lse = wide_rows(vec_ref[0:1, :], step)
    s_lse = wide_rows(vec_ref[1:2, :], step)
    weight = wide_rows(vec_ref[2:3, :], step)

    def run(t_ref, first=0):
        def body(n, carry):
            div, picked = carry
            r = pl.multiple_of(n * step, step)
            bias = mask_bias(b_ref, n)
            t = (t_ref[pl.ds(first + r, step), :] + bias).astype(F32)
            s = (s_ref[pl.ds(r, step), :] + bias).astype(F32)
            tp = jnp.exp(t - t_lse)
            sp = jnp.exp(s - s_lse)
            away = target - (base + r)
            hit = iota == jnp.broadcast_to(away[None], (step // 8, 8, lanes)).reshape(step, lanes)
            if cols is not None:
                hit = hit & (iota + (spots[at + 2] + r) < cols)
            grad = (sp - tp) - jnp.where(hit, weight, 0.0)
            g_ref[pl.ds(r, step), :] = grad.astype(BF16)
            div = div + fold(jnp.sum, tp * (t - s))
            picked = picked + fold(jnp.sum, jnp.where(hit, s, 0.0))
            return (div, picked)

        div, picked = lax.fori_loop(0, rows // step, body, (d_sum[0:8, :], d_sum[8:16, :]))
        d_sum[0:8, :] = div
        d_sum[8:16, :] = picked

    done = 0
    for ref, length in zip(pieces, spans):
        if len(pieces) == 1:
            run(ref, pl.multiple_of(g * rows, rows))
        else:
            pl.when((g >= done) & (g < done + length))(functools.partial(run, ref))
        done += length
    if last:
        @pl.when(g == pl.num_programs(0) - 1)
        def _():
            mixed = d_sum[0:8, :] - wide_rows(vec_ref[2:3, :], 8) * d_sum[8:16, :]
            d_out[...] = jnp.sum(mixed, axis=0, keepdims=True) + vec_ref[3:4, :]


def run_chunk(spots, slot, rows, pieces, student, bias, target, cols, stats=(), tokens=0, state=None, last=False):
    total, lanes = student.shape
    step = bias.shape[-1]
    lines = (rows // step,) + bias.shape[1:]
    spans = [length for _, length, _ in pieces]
    moved = pl.BlockSpec((rows, lanes), lambda g, pref: (pref[3 * (slot + g)], 0))
    after = pl.BlockSpec(lines, lambda g, pref: (pref[3 * (slot + g)] + total // rows, 0, 0))

    def fixed(height):
        return pl.BlockSpec((height, lanes), lambda g, pref: (0, 0))

    in_specs, operands = [], [spots]
    done = 0
    for array, length, local in pieces:
        def where(g, pref, done=done, length=length, local=local):
            mine = jnp.clip(g - done, 0, length - 1)
            return ((pref[3 * (slot + done + mine)] if local else mine), 0)

        held = pl.BlockSpec(memory_space=pltpu.VMEM)
        in_specs.append(held if len(pieces) == 1 else pl.BlockSpec((rows, lanes), where))
        operands.append(array)
        done += length
    in_specs += [moved, after, fixed(1)]
    operands += [student, bias, target]
    out_shape = [jax.ShapeDtypeStruct(student.shape, BF16)]
    out_specs = [moved]
    aliases = {}
    scratch = []
    if stats:
        in_specs += [fixed(8)] * len(stats)
        operands += list(stats)
        out_shape += [jax.ShapeDtypeStruct((16, lanes), F32), jax.ShapeDtypeStruct((8, lanes), F32)]
        out_specs += [fixed(16), fixed(8)]
    else:
        vec, div, grad = state
        in_specs += [fixed(8), fixed(16), pl.BlockSpec(memory_space=pl.ANY)]
        operands += [vec, div, grad]
        aliases = {len(operands) - 1: 0}
        height = 1 if last else 16
        out_shape.append(jax.ShapeDtypeStruct((height, lanes), F32))
        out_specs.append(fixed(height))
        if last:
            scratch = [pltpu.VMEM((16, lanes), F32)]

    def kernel(*refs):
        chunk_kernel(*refs, spans=spans, slot=slot, step=step, cols=cols, shares=len(stats), tokens=tokens, last=last)

    return pl.pallas_call(
        kernel,
        out_shape=tuple(out_shape),
        grid_spec=pltpu.PrefetchScalarGridSpec(
            num_scalar_prefetch=1,
            grid=(sum(spans),),
            in_specs=in_specs,
            out_specs=tuple(out_specs),
            scratch_shapes=scratch,
        ),
        input_output_aliases=aliases,
        compiler_params=pltpu.CompilerParams(dimension_semantics=("arbitrary",)),
        name="chunk",
    )(*operands)


def cut_kernel(where, t_ref, *rest, parts, held):
    outs, rest = rest[:len(parts)], rest[len(parts):]
    stops = outs if held else rest[:len(parts)]
    sems = rest[-1]
    reads, writes = [], []
    for k, (slot, start, size) in enumerate(parts):
        reads.append(pltpu.make_async_copy(t_ref.at[where[slot], pl.ds(start, size), :], stops[k], sems.at[k]))
        reads[-1].start()
    for k in range(len(parts)):
        reads[k].wait()
        if not held:
            writes.append(pltpu.make_async_copy(stops[k], outs[k], sems.at[len(parts) + k]))
            writes[-1].start()
    for copy in writes:
        copy.wait()


def cut(where, teacher, parts, held):
    lanes = teacher.shape[-1]
    space = pltpu.VMEM if held else pl.ANY
    scratch = [] if held else [pltpu.VMEM((size, lanes), BF16) for _, _, size in parts]

    def kernel(*refs):
        cut_kernel(*refs, parts=parts, held=held)

    return pl.pallas_call(
        kernel,
        out_shape=tuple(jax.ShapeDtypeStruct((size, lanes), BF16) for _, _, size in parts),
        grid_spec=pltpu.PrefetchScalarGridSpec(
            num_scalar_prefetch=1,
            grid=(1,),
            in_specs=[pl.BlockSpec(memory_space=pl.ANY)],
            out_specs=tuple(pl.BlockSpec(memory_space=space) for _ in parts),
            scratch_shapes=scratch + [pltpu.SemaphoreType.DMA((2 * len(parts),))],
        ),
        name="cut",
    )(where, teacher)


def plan(padded, voc_count):
    shifts = list(range(voc_count - 1, 0, -1))
    far = shifts[:-1] if len(shifts) > 1 else shifts
    near = shifts[len(far):]
    big = largest_part(padded, 1600)
    small = largest_part(padded, 544)
    chunked = padded == 3 * big and big == 3 * small
    pieces = []
    for index, shift in enumerate(far):
        if chunked and index == 0:
            pieces += [(shift, 0, big, big), (shift, big, 2 * big, big)]
        elif chunked and index == len(far) - 1:
            pieces += [(shift, 0, 2 * big, big), (shift, 2 * big, 2 * small, small),
                       (shift, 2 * big + 2 * small, small, small)]
        else:
            pieces.append((shift, 0, padded, big))
    late = [k for k, piece in enumerate(pieces) if len(far) > 1 and piece[0] == far[-1]]
    pieces += [(shift, 0, padded, big) for shift in near]
    early = [k for k in range(len(pieces)) if k not in late]
    return pieces, early, late, big


def body(teacher_logits, student_logits, target_ids, vocab_used):
    tok_rows, vocab_cols = teacher_logits.shape
    voc_count = lax.axis_size("voc")
    voc_index = lax.axis_index("voc")
    tok_count = lax.axis_size("tok")
    block_cols = vocab_cols // voc_count
    padded = -(-block_cols // ROWS) * ROWS
    split = padded != block_cols
    paired = voc_count & (voc_count - 1) == 0

    def partner(index, shift):
        return index ^ shift if paired else (index + shift) % voc_count

    def source(index, shift):
        return index ^ shift if paired else (index - shift) % voc_count

    def swap(value, shift):
        return lax.ppermute(value, "voc", [(i, partner(i, shift)) for i in range(voc_count)])

    def blocked(matrix):
        shaped = matrix.T.reshape(voc_count, block_cols, tok_rows)
        if split:
            shaped = jnp.pad(shaped, ((0, 0), (0, padded - block_cols), (0, 0)))
        return shaped

    teacher = blocked(teacher_logits)
    flat = teacher.reshape(voc_count * padded, tok_rows)
    student = blocked(student_logits).reshape(voc_count * padded, tok_rows)
    pieces, early, late, big = plan(padded, voc_count)

    blocks = partner(voc_index, np.array([piece[0] for piece in pieces], np.int32)).astype(jnp.int32)
    cuts = [(k, piece[1], piece[2]) for k, piece in enumerate(pieces)]
    parts = list(cut(blocks, teacher, cuts[:1], True))
    parts += list(cut(blocks, teacher, cuts[1:], False))
    arrived = []
    for k, piece in enumerate(pieces):
        arrived.append(swap(parts[k], piece[0]))

    target = target_ids.reshape(1, tok_rows)
    ids, counts = [], []
    for j in range(-(-tok_count // voc_count)):
        pairs = []
        for t in range(tok_count):
            for v in range(voc_count):
                shift = j * voc_count + v
                if shift < tok_count:
                    pairs.append((t * voc_count + v, (t + shift) % tok_count * voc_count + v))
        ids.append(lax.ppermute(target, ("tok", "voc"), pairs))
        counts.append(None if (j + 1) * voc_count <= tok_count else tok_count - j * voc_count)

    flags = vocab_used.reshape(voc_count, voc_count, block_cols)
    flags = jnp.stack([
        lax.dynamic_index_in_dim(flags, voc_index, 0, keepdims=False),
        lax.dynamic_index_in_dim(flags, voc_index, 1, keepdims=False),
    ])
    line = jnp.where(flags == 1, 0.0, NEG / LINES).astype(BF16).reshape(2 * voc_count, block_cols)
    if split:
        line = jnp.pad(line, ((0, 0), (0, padded - block_cols)), constant_values=NEG / LINES)
    step = largest_part(padded, 544)
    line = line.reshape(2 * voc_count * padded // step, 1, step)
    bias = jnp.broadcast_to(line, (line.shape[0], LINES, step))

    stats = run_stats(flat, student, bias, ids, counts, 1600)
    gathered = [stats]
    for shift in range(1, voc_count):
        gathered.append(swap(stats, shift))

    shift_of, scale, own, fixed = [], [], [], []

    def note(shift, start, size, rows):
        for at in range(start, start + size, rows):
            shift_of.extend([shift] * 3)
            scale.extend([padded // rows, voc_count * block_cols, 0])
            own.extend([0, block_cols, 0])
            fixed.extend([at // rows, at, at])
        return size // rows

    groups = []
    first = [(flat, note(0, 0, padded, big), True)]
    for k in sorted(early, key=lambda k: k < len(pieces) - 1):
        first.append((arrived[k], note(*pieces[k]), False))
    used = sum(length for _, length, _ in first)
    for k in late:
        length = note(*pieces[k])
        groups.append((used, pieces[k][3], [(arrived[k], length, False)]))
        used += length
    blocks = source(voc_index, np.array(shift_of, np.int32))
    spots = blocks * np.array(scale, np.int32) + voc_index * np.array(own, np.int32) + np.array(fixed, np.int32)
    spots = spots.astype(jnp.int32)

    cols = block_cols if split else None
    grad, div, vec = run_chunk(
        spots, 0, big, first, student, bias, target, cols, stats=gathered, tokens=tok_rows * tok_count)
    for n, (slot, rows, piece) in enumerate(groups):
        grad, div = run_chunk(
            spots, slot, rows, piece, student, bias, target, cols, state=(vec, div, grad),
            last=n == len(groups) - 1)
    if not groups:
        div = jnp.sum(div[:8] - vec[2:3] * div[8:], axis=0, keepdims=True) + vec[3:4]
    loss = div
    for shift in range(1, voc_count):
        loss = loss + swap(div, shift)
    gradient = grad.reshape(voc_count, padded, tok_rows)[:, :block_cols].reshape(vocab_cols, tok_rows).T
    return (gradient, loss.reshape(tok_rows))


def solution(mesh):
    placed = (P("tok", "voc"), P("tok", "voc"), P("tok"), P())

    step = jax.shard_map(body, mesh=mesh, in_specs=placed, out_specs=(P("tok", "voc"), P("tok")), check_vma=False)

    def whole(teacher_logits, student_logits, target_ids, vocab_used):
        run = step
        return run(teacher_logits, student_logits, target_ids, vocab_used)

    return whole
```

```python
import functools

import jax
import jax.numpy as jnp
import numpy as np
from jax import lax
from jax.experimental import pallas as pl
from jax.experimental.pallas import tpu as pltpu
from jax.sharding import PartitionSpec as P

NEG = -1e30
LOW = -3e38
ROWS = 16
LINES = 8
WAYS = 3
STEP = 544
LN2 = 0.6931471805599453
F32 = jnp.float32
BF16 = jnp.bfloat16


def largest_part(total, limit):
    best = ROWS
    for size in range(ROWS, limit + 1, ROWS):
        if total % size == 0:
            best = size
    return best


def fold(op, value, height=8):
    return op(value.reshape(-1, height, value.shape[-1]), axis=0)


def addend_rows(rows, masks, pieces):
    parts = []
    for row, mask in zip(rows, masks):
        left = -row
        part = [jnp.ones_like(row) if k == mask else jnp.zeros_like(row) for k in range(2)]
        for _ in range(pieces):
            piece = left.astype(BF16).astype(F32)
            part.append(piece)
            left = left - piece
        part.append(jnp.zeros((LINES - 2 - pieces, row.shape[1]), F32))
        parts.append(jnp.concatenate(part, axis=0))
    return jnp.concatenate(parts, axis=1).astype(BF16)


def addend(mask_ref, n, weights):
    return lax.dot_general(mask_ref[n], weights, (((0,), (0,)), ((), ())), preferred_element_type=F32)


def wide_rows(line, height):
    return jnp.broadcast_to(line, (height, line.shape[-1]))


def stats_kernel(t_ref, s_ref, m_ref, o_ref, tops, sums, block, *, step):
    g = pl.program_id(0)
    rows, lanes = t_ref.shape
    steps = rows // step
    tiles = step // ROWS

    @pl.when(g == 0)
    def _():
        tops[...] = jnp.full(tops.shape, LOW, F32)
        sums[...] = jnp.zeros(sums.shape, F32)

    def part(n):
        return pl.ds(pl.multiple_of(n * step, step), step)

    def first(n, carry):
        tops = list(carry)
        for k in range(tiles):
            tile = pl.ds(pl.multiple_of(n * step + k * ROWS, ROWS), ROWS)
            at = k % WAYS
            tops[at] = jnp.maximum(tops[at], t_ref[tile, :])
            tops[WAYS + at] = jnp.maximum(tops[WAYS + at], s_ref[tile, :])
        return tuple(tops)

    low = jnp.full((ROWS, lanes), LOW, BF16)
    highs = lax.fori_loop(0, steps, first, (low,) * (2 * WAYS))
    t_top, s_top = [
        jnp.max(functools.reduce(jnp.maximum, highs[k:k + WAYS]).astype(F32), axis=0, keepdims=True)
        for k in (0, WAYS)]
    weights = addend_rows([t_top, s_top], [0, 1], 1)

    def second(n, carry):
        both = addend(m_ref, n, weights)
        t = t_ref[part(n), :].astype(F32) + both[:, :lanes]
        s = s_ref[part(n), :].astype(F32) + both[:, lanes:]
        return (carry[0] + fold(jnp.sum, jnp.exp(t)), carry[1] + fold(jnp.sum, jnp.exp(s)))

    zero = jnp.zeros((8, lanes), F32)
    t_sum, s_sum = [
        jnp.sum(total, axis=0, keepdims=True)
        for total in lax.fori_loop(0, steps, second, (zero, zero), unroll=True)]
    block[0:1, :] = t_top
    block[1:2, :] = t_sum
    block[2:3, :] = s_top
    block[3:4, :] = s_sum

    @pl.when(jnp.min(jnp.minimum(t_sum, s_sum)) < 1e-10)
    def _():
        blank = jnp.zeros((1, lanes), F32)
        plain = addend_rows([blank, blank], [0, 1], 1)

        def masked(n):
            both = addend(m_ref, n, plain)
            return (
                t_ref[part(n), :].astype(F32) + both[:, :lanes],
                s_ref[part(n), :].astype(F32) + both[:, lanes:])

        def high(n, carry):
            return tuple(jnp.maximum(top, fold(jnp.max, value)) for top, value in zip(carry, masked(n)))

        low = jnp.full((8, lanes), LOW, F32)
        tops = [jnp.max(top, axis=0, keepdims=True) for top in lax.fori_loop(0, steps, high, (low, low))]

        def gather(n, carry):
            return tuple(
                total + fold(jnp.sum, jnp.exp(value - wide_rows(top, step)))
                for total, value, top in zip(carry, masked(n), tops))

        totals = lax.fori_loop(0, steps, gather, (zero, zero))
        for k in range(2):
            block[2 * k:2 * k + 1, :] = tops[k]
            block[2 * k + 1:2 * k + 2, :] = jnp.sum(totals[k], axis=0, keepdims=True)

    for k in range(2):
        old = tops[k:k + 1, :]
        top = block[2 * k:2 * k + 1, :]
        new = jnp.maximum(old, top)
        sums[k:k + 1, :] = (
            sums[k:k + 1, :] * jnp.exp(old - new) + block[2 * k + 1:2 * k + 2, :] * jnp.exp(top - new))
        tops[k:k + 1, :] = new

    @pl.when(g == pl.num_programs(0) - 1)
    def _():
        o_ref[...] = jnp.concatenate(
            [tops[0:1, :], sums[0:1, :], tops[1:2, :], sums[1:2, :], jnp.zeros((4, lanes), F32)], axis=0)


def run_stats(teacher, student, mask, limit):
    total, lanes = teacher.shape
    rows = largest_part(total, limit)
    count = total // rows
    near = pl.BlockSpec((rows, lanes), lambda g: (g, 0))
    step = mask.shape[-1]
    lines = (rows // step,) + mask.shape[1:]
    held = pl.BlockSpec(lines, lambda g: (g, 0, 0))

    def kernel(*refs):
        stats_kernel(*refs, step=step)

    return pl.pallas_call(
        kernel,
        out_shape=jax.ShapeDtypeStruct((8, lanes), F32),
        grid=(count,),
        in_specs=[near, near, held],
        out_specs=pl.BlockSpec((8, lanes), lambda g: (0, 0)),
        scratch_shapes=[pltpu.VMEM((8, lanes), F32)] * 3,
        compiler_params=pltpu.CompilerParams(dimension_semantics=("arbitrary",)),
        name="stats",
    )(teacher, student, mask)


def join_stats(refs, target, tokens):
    parts = [ref[...] for ref in refs]
    t_top = parts[0][0:1]
    s_top = parts[0][2:3]
    kept = parts[0][4:5]
    for part in parts[1:]:
        t_top = jnp.maximum(t_top, part[0:1])
        s_top = jnp.maximum(s_top, part[2:3])
        kept = kept + part[4:5]
    t_sum = jnp.zeros_like(t_top)
    s_sum = jnp.zeros_like(t_top)
    for part in parts:
        t_sum = t_sum + part[1:2] * jnp.exp(part[0:1] - t_top)
        s_sum = s_sum + part[3:4] * jnp.exp(part[2:3] - s_top)
    t_lse = t_top + jnp.log(t_sum)
    s_lse = s_top + jnp.log(s_sum)
    count = jnp.sum(kept, axis=1, keepdims=True)
    weight = jnp.where(target >= 0, (0.5 * tokens) / count, 0.0)
    base = (0.5 * (s_lse - t_lse) + weight * s_lse) * (1.0 / len(parts))
    blank = jnp.zeros((4, target.shape[1]), F32)
    return jnp.concatenate([t_lse + LN2, s_lse - jnp.log(0.5 + weight), weight, base, blank], axis=0)


def chunk_kernel(spots, *refs, spans, slot, step, cols, shares, tokens, last):
    pieces, refs = refs[:len(spans)], refs[len(spans):]
    s_ref, b_ref, tgt_ref = refs[:3]
    refs = refs[3:]
    g = pl.program_id(0)
    rows, lanes = s_ref.shape
    weights_ref, refs = refs[-1], refs[:-1]
    if shares:
        share_refs, (g_ref, d_out, vec_ref) = refs[:shares], refs[shares:]

        @pl.when(g == 0)
        def _():
            vec_ref[...] = join_stats(share_refs, tgt_ref[...], tokens)
            d_out[...] = jnp.zeros(d_out.shape, F32)
    else:
        vec_ref, d_in, _, g_ref, d_out = refs[:5]
        if last:
            d_sum = refs[5]
        else:
            d_sum = d_out

            @pl.when(g == 0)
            def _():
                d_out[...] = d_in[...]
    if shares:
        d_sum = d_out
    if last:
        @pl.when(g == 0)
        def _():
            d_sum[...] = d_in[...]

    @pl.when(g == 0)
    def _():
        weights_ref[...] = addend_rows([vec_ref[0:1, :], vec_ref[1:2, :]], [1, 1], 3)

    at = 3 * (slot + g)
    base = spots[at + 1]
    away = wide_rows(tgt_ref[...], 8) - lax.broadcasted_iota(jnp.int32, (8, lanes), 0)
    tile = lax.broadcasted_iota(jnp.int32, (step // 8, 8, lanes), 0)
    weight = wide_rows(vec_ref[2:3, :], step)
    weights = weights_ref[...]

    def run(t_ref, first=0):
        def body(n, carry):
            div, picked = carry
            r = pl.multiple_of(n * step, step)
            both = addend(b_ref, n, weights)
            t = t_ref[pl.ds(first + r, step), :].astype(F32)
            s = s_ref[pl.ds(r, step), :].astype(F32)
            tp = jnp.exp(t + both[:, :lanes])
            sp = jnp.exp(s + both[:, lanes:])
            gap = away - (base + r)
            line = jnp.where((gap & 7) == 0, gap >> 3, -1)
            hit = (tile == line[None]).reshape(step, lanes)
            if cols is not None:
                hit = hit & (lax.broadcasted_iota(jnp.int32, (step, lanes), 0) + (spots[at + 2] + r) < cols)
            grad = (sp - tp) - jnp.where(hit, weight, 0.0)
            g_ref[pl.ds(r, step), :] = grad.astype(BF16)
            div = div + fold(jnp.sum, tp * (t - s))
            picked = picked + fold(jnp.sum, jnp.where(hit, s, 0.0))
            return (div, picked)

        div, picked = lax.fori_loop(0, rows // step, body, (d_sum[0:8, :], d_sum[8:16, :]), unroll=True)
        d_sum[0:8, :] = div
        d_sum[8:16, :] = picked

    done = 0
    for ref, length in zip(pieces, spans):
        if len(pieces) == 1:
            run(ref, pl.multiple_of(g * rows, rows))
        else:
            pl.when((g >= done) & (g < done + length))(functools.partial(run, ref))
        done += length
    if last:
        @pl.when(g == pl.num_programs(0) - 1)
        def _():
            mixed = d_sum[0:8, :] - wide_rows(vec_ref[2:3, :], 8) * d_sum[8:16, :]
            d_out[...] = jnp.sum(mixed, axis=0, keepdims=True) + vec_ref[3:4, :]


def run_chunk(spots, slot, rows, pieces, student, bias, target, cols, stats=(), tokens=0, state=None, last=False):
    _, lanes = student.shape
    step = bias.shape[-1]
    lines = (rows // step,) + bias.shape[1:]
    spans = [length for _, length, _ in pieces]
    moved = pl.BlockSpec((rows, lanes), lambda g, pref: (pref[3 * (slot + g)], 0))
    after = pl.BlockSpec(lines, lambda g, pref: (pref[3 * (slot + g)], 0, 0))

    def fixed(height):
        return pl.BlockSpec((height, lanes), lambda g, pref: (0, 0))

    in_specs, operands = [], [spots]
    done = 0
    for array, length, local in pieces:
        def where(g, pref, done=done, length=length, local=local):
            mine = jnp.clip(g - done, 0, length - 1)
            return ((pref[3 * (slot + done + mine)] if local else mine), 0)

        held = pl.BlockSpec(memory_space=pltpu.VMEM)
        in_specs.append(held if len(pieces) == 1 else pl.BlockSpec((rows, lanes), where))
        operands.append(array)
        done += length
    in_specs += [moved, after, fixed(1)]
    operands += [student, bias, target]
    out_shape = [jax.ShapeDtypeStruct(student.shape, BF16)]
    out_specs = [moved]
    aliases = {}
    scratch = []
    if stats:
        in_specs += [fixed(8)] * len(stats)
        operands += list(stats)
        out_shape += [jax.ShapeDtypeStruct((16, lanes), F32), jax.ShapeDtypeStruct((8, lanes), F32)]
        out_specs += [fixed(16), fixed(8)]
    else:
        vec, div, grad = state
        in_specs += [fixed(8), fixed(16), pl.BlockSpec(memory_space=pl.ANY)]
        operands += [vec, div, grad]
        aliases = {len(operands) - 1: 0}
        height = 1 if last else 16
        out_shape.append(jax.ShapeDtypeStruct((height, lanes), F32))
        out_specs.append(fixed(height))
        if last:
            scratch = [pltpu.VMEM((16, lanes), F32)]
    scratch.append(pltpu.VMEM((LINES, 2 * lanes), BF16))

    def kernel(*refs):
        chunk_kernel(*refs, spans=spans, slot=slot, step=step, cols=cols, shares=len(stats), tokens=tokens, last=last)

    return pl.pallas_call(
        kernel,
        out_shape=tuple(out_shape),
        grid_spec=pltpu.PrefetchScalarGridSpec(
            num_scalar_prefetch=1,
            grid=(sum(spans),),
            in_specs=in_specs,
            out_specs=tuple(out_specs),
            scratch_shapes=scratch,
        ),
        input_output_aliases=aliases,
        compiler_params=pltpu.CompilerParams(dimension_semantics=("arbitrary",)),
        name="chunk",
    )(*operands)


def cut_kernel(t_ref, *rest, parts, held, partner):
    outs, rest = rest[:len(parts)], rest[len(parts):]
    stops = outs if held else rest[:len(parts)]
    sems = rest[-1]
    reads, writes = [], []
    me = lax.axis_index("voc")
    for k, (shift, start, size) in enumerate(parts):
        block = partner(me, shift)
        reads.append(pltpu.make_async_copy(t_ref.at[block, pl.ds(start, size), :], stops[k], sems.at[k]))
        reads[-1].start()
    for k in range(len(parts)):
        reads[k].wait()
        if not held:
            writes.append(pltpu.make_async_copy(stops[k], outs[k], sems.at[len(parts) + k]))
            writes[-1].start()
    for copy in writes:
        copy.wait()


def cut(teacher, parts, held, partner):
    lanes = teacher.shape[-1]
    space = pltpu.VMEM if held else pl.ANY
    scratch = [] if held else [pltpu.VMEM((size, lanes), BF16) for _, _, size in parts]

    def kernel(*refs):
        cut_kernel(*refs, parts=parts, held=held, partner=partner)

    return pl.pallas_call(
        kernel,
        out_shape=tuple(jax.ShapeDtypeStruct((size, lanes), BF16) for _, _, size in parts),
        in_specs=[pl.BlockSpec(memory_space=pl.ANY)],
        out_specs=tuple(pl.BlockSpec(memory_space=space) for _ in parts),
        scratch_shapes=scratch + [pltpu.SemaphoreType.DMA((2 * len(parts),))],
        name="cut",
    )(teacher)


def plan(padded, voc_count):
    shifts = list(range(voc_count - 1, 0, -1))
    far = shifts[:-1] if len(shifts) > 1 else shifts
    near = shifts[len(far):]
    big = largest_part(padded, 1600)
    small = largest_part(padded, 544)
    chunked = padded == 3 * big and big == 3 * small
    pieces = []
    for index, shift in enumerate(far):
        if chunked and index == 0:
            pieces += [(shift, 0, big, big), (shift, big, 2 * big, big)]
        elif chunked and index == len(far) - 1:
            pieces += [(shift, 0, big, big), (shift, big, big, big), (shift, 2 * big, 2 * small, small),
                       (shift, 2 * big + 2 * small, small, small)]
        else:
            pieces.append((shift, 0, padded, big))
    late = [k for k, piece in enumerate(pieces) if len(far) > 1 and piece[0] == far[-1] and (piece[1] or not chunked)]
    pieces += [(shift, 0, padded, big) for shift in near]
    early = [k for k in range(len(pieces)) if k not in late]
    return pieces, early, late, big


def body(teacher_logits, student_logits, target_ids, vocab_used):
    tok_rows, vocab_cols = teacher_logits.shape
    voc_count = lax.axis_size("voc")
    voc_index = lax.axis_index("voc")
    tok_count = lax.axis_size("tok")
    block_cols = vocab_cols // voc_count
    padded = -(-block_cols // ROWS) * ROWS
    split = padded != block_cols
    paired = voc_count & (voc_count - 1) == 0

    def partner(index, shift):
        return index ^ shift if paired else (index + shift) % voc_count

    def source(index, shift):
        return index ^ shift if paired else (index - shift) % voc_count

    def swap(value, shift):
        return lax.ppermute(value, "voc", [(i, partner(i, shift)) for i in range(voc_count)])

    def blocked(matrix):
        shaped = matrix.T.reshape(voc_count, block_cols, tok_rows)
        if split:
            shaped = jnp.pad(shaped, ((0, 0), (0, padded - block_cols), (0, 0)))
        return shaped

    teacher = blocked(teacher_logits)
    flat = teacher.reshape(voc_count * padded, tok_rows)
    student = blocked(student_logits).reshape(voc_count * padded, tok_rows)
    pieces, early, late, big = plan(padded, voc_count)

    cuts = [piece[:3] for piece in pieces]
    parts = list(cut(teacher, cuts[:1], True, partner))
    parts += list(cut(teacher, cuts[1:], False, partner))
    arrived = []
    for k, piece in enumerate(pieces):
        arrived.append(swap(parts[k], piece[0]))

    target = target_ids.reshape(1, tok_rows)
    kept = (target >= 0).astype(F32)
    merged = 1
    step = 0
    while tok_count // merged > voc_count:
        pairs = [(i, i ^ merged) for i in range(tok_count)]
        if step == 0:
            kept = kept + (lax.ppermute(target, "tok", pairs) >= 0).astype(F32)
        else:
            kept = kept + lax.ppermute(kept, "tok", pairs)
        merged *= 2
        step += 1
    left = tok_count // merged
    pairs = [
        (t * voc_count + v, ((t // merged + v) % left * merged + t % merged) * voc_count + v)
        for t in range(tok_count) for v in range(left)
    ]
    kept = lax.ppermute(kept, ("tok", "voc"), pairs)

    flags = vocab_used.reshape(voc_count, voc_count, block_cols)
    flags = jnp.stack([
        lax.dynamic_index_in_dim(flags, voc_index, 0, keepdims=False),
        lax.dynamic_index_in_dim(flags, voc_index, 1, keepdims=False),
    ])
    line = jnp.where(flags == 1, 0.0, NEG).astype(BF16).reshape(2 * voc_count, block_cols)
    if split:
        line = jnp.pad(line, ((0, 0), (0, padded - block_cols)), constant_values=NEG)
    step = largest_part(padded, STEP)
    line = line.reshape(2, voc_count * padded // step, 1, step)
    kind = lax.broadcasted_iota(jnp.int32, (1, LINES, 1), 1)
    ones = jnp.where(kind < 5, 1.0, 0.0).astype(BF16)
    bias = jnp.where(kind == 0, line[0], jnp.where(kind == 1, line[1], ones))

    stats = run_stats(flat, student, bias, 1600)
    stats = jnp.concatenate([stats[:4], kept, stats[5:]], axis=0)
    gathered = [stats]
    for shift in range(1, voc_count):
        gathered.append(swap(stats, shift))

    shift_of, scale, own, fixed = [], [], [], []

    def note(shift, start, size, rows):
        for at in range(start, start + size, rows):
            shift_of.extend([shift] * 3)
            scale.extend([padded // rows, voc_count * block_cols, 0])
            own.extend([0, block_cols, 0])
            fixed.extend([at // rows, at, at])
        return size // rows

    groups = []
    first = [(flat, note(0, 0, padded, big), True)]
    for k in sorted(early, key=lambda k: k < len(pieces) - 1):
        first.append((arrived[k], note(*pieces[k]), False))
    used = sum(length for _, length, _ in first)
    for k in late:
        length = note(*pieces[k])
        groups.append((used, pieces[k][3], [(arrived[k], length, False)]))
        used += length
    blocks = source(voc_index, np.array(shift_of, np.int32))
    spots = blocks * np.array(scale, np.int32) + voc_index * np.array(own, np.int32) + np.array(fixed, np.int32)
    spots = spots.astype(jnp.int32)

    cols = block_cols if split else None
    grad, div, vec = run_chunk(
        spots, 0, big, first, student, bias, target, cols, stats=gathered, tokens=tok_rows * tok_count)
    for n, (slot, rows, piece) in enumerate(groups):
        grad, div = run_chunk(
            spots, slot, rows, piece, student, bias, target, cols, state=(vec, div, grad),
            last=n == len(groups) - 1)
    if not groups:
        div = jnp.sum(div[:8] - vec[2:3] * div[8:], axis=0, keepdims=True) + vec[3:4]
    loss = div
    for shift in range(1, voc_count):
        loss = loss + swap(div, shift)
    gradient = grad.reshape(voc_count, padded, tok_rows)[:, :block_cols].reshape(vocab_cols, tok_rows).T
    return (gradient, loss.reshape(tok_rows))


def solution(mesh):
    placed = (P("tok", "voc"), P("tok", "voc"), P("tok"), P())

    step = jax.shard_map(body, mesh=mesh, in_specs=placed, out_specs=(P("tok", "voc"), P("tok")), check_vma=False)

    def whole(teacher_logits, student_logits, target_ids, vocab_used):
        run = step
        return run(teacher_logits, student_logits, target_ids, vocab_used)

    return whole
```

```python
import functools

import jax
import jax.numpy as jnp
import numpy as np
from jax import lax
from jax.experimental import pallas as pl
from jax.experimental.pallas import tpu as pltpu
from jax.sharding import PartitionSpec as P

NEG = -1e30
LOW = -3e38
ROWS = 16
LINES = 8
HELD_BYTES = 3 * 2**20
WAYS = 3
AHEAD = 1
STEP = 544
LN2 = 0.6931471805599453
F32 = jnp.float32
BF16 = jnp.bfloat16


def largest_part(total, limit):
    best = ROWS
    for size in range(ROWS, limit + 1, ROWS):
        if total % size == 0:
            best = size
    return best


def fold(op, value, height=8):
    return op(value.reshape(-1, height, value.shape[-1]), axis=0)


def addend_rows(rows, masks, pieces):
    parts = []
    for row, mask in zip(rows, masks):
        left = -row
        part = [jnp.ones_like(row) if k == mask else jnp.zeros_like(row) for k in range(2)]
        for _ in range(pieces):
            piece = left.astype(BF16).astype(F32)
            part.append(piece)
            left = left - piece
        part.append(jnp.zeros((LINES - 2 - pieces, row.shape[1]), F32))
        parts.append(jnp.concatenate(part, axis=0))
    return jnp.concatenate(parts, axis=1).astype(BF16)


def addend(mask_ref, n, weights):
    return lax.dot_general(mask_ref[n], weights, (((0,), (0,)), ((), ())), preferred_element_type=F32)


def wide_rows(line, height):
    return jnp.broadcast_to(line, (height, line.shape[-1]))


def stats_kernel(t_ref, s_ref, m_ref, o_ref, tops, sums, block, *, step):
    g = pl.program_id(0)
    rows, lanes = t_ref.shape
    steps = rows // step
    tiles = step // ROWS

    @pl.when(g == 0)
    def _():
        tops[...] = jnp.full(tops.shape, LOW, F32)
        sums[...] = jnp.zeros(sums.shape, F32)

    def part(n):
        return pl.ds(pl.multiple_of(n * step, step), step)

    def first(n, carry):
        tops = list(carry)
        for k in range(tiles):
            tile = pl.ds(pl.multiple_of(n * step + k * ROWS, ROWS), ROWS)
            at = k % WAYS
            tops[at] = jnp.maximum(tops[at], t_ref[tile, :].astype(F32))
            tops[WAYS + at] = jnp.maximum(tops[WAYS + at], s_ref[tile, :].astype(F32))
        return tuple(tops)

    low = jnp.full((ROWS, lanes), LOW, F32)
    highs = lax.fori_loop(0, steps, first, (low,) * (2 * WAYS), unroll=True)
    t_top, s_top = [
        jnp.max(functools.reduce(jnp.maximum, highs[k:k + WAYS]), axis=0, keepdims=True)
        for k in (0, WAYS)]
    weights = addend_rows([t_top, s_top], [0, 1], 1)

    def second(n, carry):
        both = addend(m_ref, n, weights)
        t = t_ref[part(n), :].astype(F32) + both[:, :lanes]
        s = s_ref[part(n), :].astype(F32) + both[:, lanes:]
        return (carry[0] + fold(jnp.sum, jnp.exp(t)), carry[1] + fold(jnp.sum, jnp.exp(s)))

    zero = jnp.zeros((8, lanes), F32)
    t_sum, s_sum = [
        jnp.sum(total, axis=0, keepdims=True)
        for total in lax.fori_loop(0, steps, second, (zero, zero), unroll=True)]
    block[0:1, :] = t_top
    block[1:2, :] = t_sum
    block[2:3, :] = s_top
    block[3:4, :] = s_sum

    @pl.when(jnp.min(jnp.minimum(t_sum, s_sum)) < 1e-10)
    def _():
        blank = jnp.zeros((1, lanes), F32)
        plain = addend_rows([blank, blank], [0, 1], 1)

        def masked(n):
            both = addend(m_ref, n, plain)
            return (
                t_ref[part(n), :].astype(F32) + both[:, :lanes],
                s_ref[part(n), :].astype(F32) + both[:, lanes:])

        def high(n, carry):
            return tuple(jnp.maximum(top, fold(jnp.max, value)) for top, value in zip(carry, masked(n)))

        low = jnp.full((8, lanes), LOW, F32)
        tops = [jnp.max(top, axis=0, keepdims=True) for top in lax.fori_loop(0, steps, high, (low, low))]

        def gather(n, carry):
            return tuple(
                total + fold(jnp.sum, jnp.exp(value - wide_rows(top, step)))
                for total, value, top in zip(carry, masked(n), tops))

        totals = lax.fori_loop(0, steps, gather, (zero, zero))
        for k in range(2):
            block[2 * k:2 * k + 1, :] = tops[k]
            block[2 * k + 1:2 * k + 2, :] = jnp.sum(totals[k], axis=0, keepdims=True)

    for k in range(2):
        old = tops[k:k + 1, :]
        top = block[2 * k:2 * k + 1, :]
        new = jnp.maximum(old, top)
        sums[k:k + 1, :] = (
            sums[k:k + 1, :] * jnp.exp(old - new) + block[2 * k + 1:2 * k + 2, :] * jnp.exp(top - new))
        tops[k:k + 1, :] = new

    @pl.when(g == pl.num_programs(0) - 1)
    def _():
        o_ref[...] = jnp.concatenate(
            [tops[0:1, :], sums[0:1, :], tops[1:2, :], sums[1:2, :], jnp.zeros((4, lanes), F32)], axis=0)


def run_stats(teacher, student, mask, limit):
    total, lanes = teacher.shape
    rows = largest_part(total, limit)
    count = total // rows
    near = pl.BlockSpec((rows, lanes), lambda g: (g, 0))
    step = mask.shape[-1]
    lines = (rows // step,) + mask.shape[1:]
    held = pl.BlockSpec(lines, lambda g: (g, 0, 0))

    def kernel(*refs):
        stats_kernel(*refs, step=step)

    return pl.pallas_call(
        kernel,
        out_shape=jax.ShapeDtypeStruct((8, lanes), F32),
        grid=(count,),
        in_specs=[near, near, held],
        out_specs=pl.BlockSpec((8, lanes), lambda g: (0, 0)),
        scratch_shapes=[pltpu.VMEM((8, lanes), F32)] * 3,
        compiler_params=pltpu.CompilerParams(dimension_semantics=("arbitrary",)),
        name="stats",
    )(teacher, student, mask)


def join_stats(refs, target, tokens):
    parts = [ref[...] for ref in refs]
    t_top = parts[0][0:1]
    s_top = parts[0][2:3]
    kept = parts[0][4:5]
    for part in parts[1:]:
        t_top = jnp.maximum(t_top, part[0:1])
        s_top = jnp.maximum(s_top, part[2:3])
        kept = kept + part[4:5]
    t_sum = jnp.zeros_like(t_top)
    s_sum = jnp.zeros_like(t_top)
    for part in parts:
        t_sum = t_sum + part[1:2] * jnp.exp(part[0:1] - t_top)
        s_sum = s_sum + part[3:4] * jnp.exp(part[2:3] - s_top)
    t_lse = t_top + jnp.log(t_sum)
    s_lse = s_top + jnp.log(s_sum)
    count = jnp.sum(kept, axis=1, keepdims=True)
    weight = jnp.where(target >= 0, (0.5 * tokens) / count, 0.0)
    base = (0.5 * (s_lse - t_lse) + weight * s_lse) * (1.0 / len(parts))
    blank = jnp.zeros((4, target.shape[1]), F32)
    return jnp.concatenate([t_lse + LN2, s_lse - jnp.log(0.5 + weight), weight, base, blank], axis=0)


def chunk_kernel(spots, *refs, spans, slot, step, cols, shares, tokens):
    pieces, refs = refs[:len(spans)], refs[len(spans):]
    s_ref, b_ref, tgt_ref = refs[:3]
    refs = refs[3:]
    g = pl.program_id(0)
    rows, lanes = s_ref.shape
    weights_ref, refs = refs[-1], refs[:-1]
    if shares:
        share_refs, (g_ref, d_out, vec_ref) = refs[:shares], refs[shares:]

        @pl.when(g == 0)
        def _():
            vec_ref[...] = join_stats(share_refs, tgt_ref[...], tokens)
            d_out[...] = jnp.zeros(d_out.shape, F32)
    else:
        vec_ref, d_in, _, g_ref, d_out = refs

        @pl.when(g == 0)
        def _():
            d_out[...] = d_in[...]

    @pl.when(g == 0)
    def _():
        weights_ref[...] = addend_rows([vec_ref[0:1, :], vec_ref[1:2, :]], [1, 1], 3)

    at = 3 * (slot + g)
    base = spots[at + 1]
    away = wide_rows(tgt_ref[...], 8) - lax.broadcasted_iota(jnp.int32, (8, lanes), 0)
    tile = lax.broadcasted_iota(jnp.int32, (step // 8, 8, lanes), 0)
    weight = wide_rows(vec_ref[2:3, :], step)
    weights = weights_ref[...]

    def run(t_ref, first=0):
        def body(n, carry):
            div, picked = carry
            r = pl.multiple_of(n * step, step)
            both = addend(b_ref, n, weights)
            t = t_ref[pl.ds(first + r, step), :].astype(F32)
            s = s_ref[pl.ds(r, step), :].astype(F32)
            tp = jnp.exp(t + both[:, :lanes])
            sp = jnp.exp(s + both[:, lanes:])
            gap = away - (base + r)
            line = jnp.where((gap & 7) == 0, gap >> 3, -1)
            hit = (tile == line[None]).reshape(step, lanes)
            if cols is not None:
                hit = hit & (lax.broadcasted_iota(jnp.int32, (step, lanes), 0) + (spots[at + 2] + r) < cols)
            grad = (sp - tp) - jnp.where(hit, weight, 0.0)
            g_ref[pl.ds(r, step), :] = grad.astype(BF16)
            div = div + fold(jnp.sum, tp * (t - s))
            picked = picked + fold(jnp.sum, jnp.where(hit, s, 0.0))
            return (div, picked)

        div, picked = lax.fori_loop(0, rows // step, body, (d_out[0:8, :], d_out[8:16, :]), unroll=True)
        d_out[0:8, :] = div
        d_out[8:16, :] = picked

    done = 0
    for ref, (length, held) in zip(pieces, spans):
        first = pl.multiple_of((g - done) * rows, rows) if held else 0
        if len(pieces) == 1:
            run(ref, first)
        else:
            pl.when((g >= done) & (g < done + length))(functools.partial(run, ref, first))
        done += length


def run_chunk(spots, slot, rows, pieces, student, bias, target, cols, stats=(), tokens=0, state=None):
    _, lanes = student.shape
    step = bias.shape[-1]
    lines = (rows // step,) + bias.shape[1:]
    spans = [(length, local is None) for _, length, local in pieces]
    moved = pl.BlockSpec((rows, lanes), lambda g, pref: (pref[3 * (slot + g)], 0))
    after = pl.BlockSpec(lines, lambda g, pref: (pref[3 * (slot + g)], 0, 0))

    def fixed(height):
        return pl.BlockSpec((height, lanes), lambda g, pref: (0, 0))

    in_specs, operands = [], [spots]
    done = 0
    for array, length, local in pieces:
        def where(g, pref, done=done, length=length, local=local):
            mine = jnp.clip(g - done, 0, length - 1)
            return ((pref[3 * (slot + done + mine)] if local else mine), 0)

        if local is None:
            in_specs.append(pl.BlockSpec(memory_space=pltpu.VMEM))
            array = pltpu.with_memory_space_constraint(array, pltpu.VMEM)
        else:
            in_specs.append(pl.BlockSpec((rows, lanes), where))
        operands.append(array)
        done += length
    in_specs += [moved, after, fixed(1)]
    operands += [student, bias, target]
    out_shape = [jax.ShapeDtypeStruct(student.shape, BF16)]
    out_specs = [moved]
    aliases = {}
    if stats:
        in_specs += [fixed(8)] * len(stats)
        operands += list(stats)
        out_shape += [jax.ShapeDtypeStruct((16, lanes), F32), jax.ShapeDtypeStruct((8, lanes), F32)]
        out_specs += [fixed(16), fixed(8)]
    else:
        vec, div, grad = state
        in_specs += [fixed(8), fixed(16), pl.BlockSpec(memory_space=pl.ANY)]
        operands += [vec, div, grad]
        aliases = {len(operands) - 1: 0}
        out_shape.append(jax.ShapeDtypeStruct((16, lanes), F32))
        out_specs.append(fixed(16))
    scratch = [pltpu.VMEM((LINES, 2 * lanes), BF16)]

    def kernel(*refs):
        chunk_kernel(*refs, spans=spans, slot=slot, step=step, cols=cols, shares=len(stats), tokens=tokens)

    return pl.pallas_call(
        kernel,
        out_shape=tuple(out_shape),
        grid_spec=pltpu.PrefetchScalarGridSpec(
            num_scalar_prefetch=1,
            grid=(sum(length for length, _ in spans),),
            in_specs=in_specs,
            out_specs=tuple(out_specs),
            scratch_shapes=scratch,
        ),
        input_output_aliases=aliases,
        compiler_params=pltpu.CompilerParams(dimension_semantics=("arbitrary",)),
        name="chunk",
    )(*operands)


def hits(base, r, tgt_ref, step, lanes, limit):
    gap = wide_rows(tgt_ref[...], 8) - lax.broadcasted_iota(jnp.int32, (8, lanes), 0) - (base + r)
    line = jnp.where((gap & 7) == 0, gap >> 3, -1)
    tile = lax.broadcasted_iota(jnp.int32, (step // 8, 8, lanes), 0)
    hit = (tile == line[None]).reshape(step, lanes)
    if limit is not None:
        hit = hit & (lax.broadcasted_iota(jnp.int32, (step, lanes), 0) < limit - r)
    return hit


def tail_sum_kernel(t_ref, s_ref, m_ref, vec_ref, tgt_ref, d_ref, o_ref, *, first_id, limit):
    rows, lanes = t_ref.shape
    step = m_ref.shape[-1]
    weights = addend_rows([vec_ref[0:1, :]], [1], 3)
    base = first_id()
    div = jnp.zeros((8, lanes), F32)
    picked = jnp.zeros((8, lanes), F32)
    for n in range(rows // step):
        t = t_ref[n * step:(n + 1) * step, :].astype(F32)
        s = s_ref[n * step:(n + 1) * step, :].astype(F32)
        tp = jnp.exp(t + addend(m_ref, n, weights))
        div = div + fold(jnp.sum, tp * (t - s))
        hit = hits(base, n * step, tgt_ref, step, lanes, limit)
        picked = picked + fold(jnp.sum, jnp.where(hit, s, 0.0))
    total = div - wide_rows(vec_ref[2:3, :], 8) * picked
    o_ref[...] = jnp.sum(total, axis=0, keepdims=True) + d_ref[...]


def tail_grad_kernel(t_ref, s_ref, m_ref, vec_ref, tgt_ref, _, g_ref, out, sems, *, first_id, first_row, limit):
    rows, lanes = t_ref.shape
    step = m_ref.shape[-1]
    weights = addend_rows([vec_ref[0:1, :], vec_ref[1:2, :]], [1, 1], 3)
    weight = wide_rows(vec_ref[2:3, :], step)
    base = first_id()
    row = first_row()
    copies = []
    for n in range(rows // step):
        part = pl.ds(n * step, step)
        both = addend(m_ref, n, weights)
        tp = jnp.exp(t_ref[part, :].astype(F32) + both[:, :lanes])
        sp = jnp.exp(s_ref[part, :].astype(F32) + both[:, lanes:])
        hit = hits(base, n * step, tgt_ref, step, lanes, limit)
        out[part, :] = ((sp - tp) - jnp.where(hit, weight, 0.0)).astype(BF16)
        place = pl.ds(pl.multiple_of(row + n * step, ROWS), step)
        copies.append(pltpu.make_async_copy(out.at[part, :], g_ref.at[place, :], sems.at[n]))
        copies[-1].start()
    for copy in copies:
        copy.wait()


def held(value):
    return pltpu.with_memory_space_constraint(value, pltpu.VMEM)


def run_tail_sum(operands, first_id, limit):
    lanes = operands[0].shape[1]

    def kernel(*refs):
        tail_sum_kernel(*refs, first_id=first_id, limit=limit)

    return pl.pallas_call(
        kernel,
        out_shape=jax.ShapeDtypeStruct((1, lanes), F32),
        in_specs=[pl.BlockSpec(memory_space=pltpu.VMEM)] * len(operands),
        out_specs=pl.BlockSpec(memory_space=pltpu.VMEM),
        name="tail_sum",
    )(*[held(value) for value in operands])


def run_tail_grad(operands, grad, first_id, first_row, limit):
    rows, lanes = operands[0].shape
    step = operands[2].shape[-1]

    def kernel(*refs):
        tail_grad_kernel(*refs, first_id=first_id, first_row=first_row, limit=limit)

    return pl.pallas_call(
        kernel,
        out_shape=jax.ShapeDtypeStruct(grad.shape, grad.dtype),
        in_specs=[pl.BlockSpec(memory_space=pltpu.VMEM)] * len(operands) + [pl.BlockSpec(memory_space=pl.ANY)],
        out_specs=pl.BlockSpec(memory_space=pl.ANY),
        scratch_shapes=[pltpu.VMEM((rows, lanes), BF16), pltpu.SemaphoreType.DMA((rows // step,))],
        input_output_aliases={len(operands): 0},
        name="tail_grad",
    )(*[held(value) for value in operands], grad)


def cut_kernel(t_ref, *rest, parts, held, partner):
    outs, rest = rest[:len(parts)], rest[len(parts):]
    stops = outs if held else rest[:len(parts)]
    sems = rest[-1]
    reads, writes = [], []
    me = lax.axis_index("voc")
    for k, (shift, start, size) in enumerate(parts):
        block = partner(me, shift)
        reads.append(pltpu.make_async_copy(t_ref.at[block, pl.ds(start, size), :], stops[k], sems.at[k]))
        reads[-1].start()
    for k in range(len(parts)):
        reads[k].wait()
        if not held:
            writes.append(pltpu.make_async_copy(stops[k], outs[k], sems.at[len(parts) + k]))
            writes[-1].start()
    for copy in writes:
        copy.wait()


def cut(teacher, parts, held, partner):
    lanes = teacher.shape[-1]
    space = pltpu.VMEM if held else pl.ANY
    scratch = [] if held else [pltpu.VMEM((size, lanes), BF16) for _, _, size in parts]

    def kernel(*refs):
        cut_kernel(*refs, parts=parts, held=held, partner=partner)

    return pl.pallas_call(
        kernel,
        out_shape=tuple(jax.ShapeDtypeStruct((size, lanes), BF16) for _, _, size in parts),
        in_specs=[pl.BlockSpec(memory_space=pl.ANY)],
        out_specs=tuple(pl.BlockSpec(memory_space=space) for _ in parts),
        scratch_shapes=scratch + [pltpu.SemaphoreType.DMA((2 * len(parts),))],
        name="cut",
    )(teacher)


def plan(padded, voc_count):
    shifts = list(range(voc_count - 1, 0, -1))
    far = shifts[:-1] if len(shifts) > 1 else shifts
    near = shifts[len(far):]
    big = largest_part(padded, 1600)
    small = largest_part(padded, 544)
    chunked = padded == 3 * big and big == 3 * small
    pieces = []
    for index, shift in enumerate(far):
        if chunked and index == 0:
            pieces += [(shift, 0, big, big), (shift, big, 2 * big, big)]
        elif chunked and index == len(far) - 1:
            pieces += [(shift, 0, AHEAD * small, small), (shift, AHEAD * small, (6 - AHEAD) * small, small),
                       (shift, 2 * big, big, big)]
        else:
            pieces.append((shift, 0, padded, big))
    late = [k for k, piece in enumerate(pieces) if len(far) > 1 and piece[0] == far[-1] and (piece[1] or not chunked)]
    pieces += [(shift, 0, padded, big) for shift in near]
    early = [k for k in range(len(pieces)) if k not in late]
    return pieces, early, late, big


def body(teacher_logits, student_logits, target_ids, vocab_used):
    tok_rows, vocab_cols = teacher_logits.shape
    voc_count = lax.axis_size("voc")
    voc_index = lax.axis_index("voc")
    tok_count = lax.axis_size("tok")
    block_cols = vocab_cols // voc_count
    padded = -(-block_cols // ROWS) * ROWS
    split = padded != block_cols
    paired = voc_count & (voc_count - 1) == 0

    def partner(index, shift):
        return index ^ shift if paired else (index + shift) % voc_count

    def source(index, shift):
        return index ^ shift if paired else (index - shift) % voc_count

    def swap(value, shift):
        return lax.ppermute(value, "voc", [(i, partner(i, shift)) for i in range(voc_count)])

    def blocked(matrix):
        shaped = matrix.T.reshape(voc_count, block_cols, tok_rows)
        if split:
            shaped = jnp.pad(shaped, ((0, 0), (0, padded - block_cols), (0, 0)))
        return shaped

    teacher = blocked(teacher_logits)
    flat = teacher.reshape(voc_count * padded, tok_rows)
    student = blocked(student_logits).reshape(voc_count * padded, tok_rows)
    pieces, early, late, big = plan(padded, voc_count)

    cuts = [piece[:3] for piece in pieces]
    parts = list(cut(teacher, cuts[:1], True, partner))
    parts += list(cut(teacher, cuts[1:], False, partner))
    arrived = []
    for k, piece in enumerate(pieces):
        arrived.append(swap(parts[k], piece[0]))

    target = target_ids.reshape(1, tok_rows)
    kept = (target >= 0).astype(F32)
    merged = 1
    step = 0
    while tok_count // merged > voc_count:
        pairs = [(i, i ^ merged) for i in range(tok_count)]
        if step == 0:
            kept = kept + (lax.ppermute(target, "tok", pairs) >= 0).astype(F32)
        else:
            kept = kept + lax.ppermute(kept, "tok", pairs)
        merged *= 2
        step += 1
    left = tok_count // merged
    even = left & (left - 1) == 0
    pairs = [
        (t * voc_count + v,
         ((t // merged ^ v if even else (t // merged + v) % left) * merged + t % merged) * voc_count + v)
        for t in range(tok_count) for v in range(left)
    ]
    kept = lax.ppermute(kept, ("tok", "voc"), pairs)

    flags = vocab_used.reshape(voc_count, voc_count, block_cols)
    flags = jnp.stack([
        lax.dynamic_index_in_dim(flags, voc_index, 0, keepdims=False),
        lax.dynamic_index_in_dim(flags, voc_index, 1, keepdims=False),
    ])
    line = jnp.where(flags == 1, 0.0, NEG).astype(BF16).reshape(2 * voc_count, block_cols)
    if split:
        line = jnp.pad(line, ((0, 0), (0, padded - block_cols)), constant_values=NEG)
    step = largest_part(padded, STEP)
    line = line.reshape(2, voc_count * padded // step, 1, step)
    kind = lax.broadcasted_iota(jnp.int32, (1, LINES, 1), 1)
    ones = jnp.where(kind < 5, 1.0, 0.0).astype(BF16)
    bias = jnp.where(kind == 0, line[0], jnp.where(kind == 1, line[1], ones))

    stats = run_stats(flat, student, bias, 1600)
    stats = jnp.where(lax.broadcasted_iota(jnp.int32, stats.shape, 0) == 4, kept, stats)
    gathered = [stats]
    for shift in range(1, voc_count):
        gathered.append(swap(stats, shift))

    shift_of, scale, own, fixed = [], [], [], []

    def note(shift, start, size, rows):
        for at in range(start, start + size, rows):
            shift_of.extend([shift] * 3)
            scale.extend([padded // rows, voc_count * block_cols, 0])
            own.extend([0, block_cols, 0])
            fixed.extend([at // rows, at, at])
        return size // rows

    groups = []
    held = [pair[1] for pair in sorted((piece[2], k) for k, piece in enumerate(pieces))]
    held = late + [k for k in reversed(held) if k in early]
    size = 0
    for n, k in enumerate(held):
        size += pieces[k][2] * tok_rows * 2
        if size > HELD_BYTES:
            held = held[:n]
            break
    first = [(flat, note(0, 0, padded, big), True)]
    for k in sorted(early, key=lambda k: k < len(pieces) - 1):
        if pieces[k][3] == big:
            first.append((arrived[k], note(*pieces[k]), None if k in held else False))
    used = sum(length for _, length, _ in first)
    apart = [k for k in early if pieces[k][3] != big]
    for k in late:
        group = []
        start = used
        for j in apart + [k]:
            group.append((arrived[j], note(*pieces[j]), None if j in held else False))
            used += group[-1][1]
        groups.append((start, pieces[k][3], group))
        apart = []
    blocks = source(voc_index, np.array(shift_of, np.int32))
    spots = blocks * np.array(scale, np.int32) + voc_index * np.array(own, np.int32) + np.array(fixed, np.int32)
    spots = spots.astype(jnp.int32)

    cols = block_cols if split else None
    grad, div, vec = run_chunk(
        spots, 0, big, first, student, bias, target, cols, stats=gathered, tokens=tok_rows * tok_count)
    for slot, rows, piece in groups[:-1]:
        grad, div = run_chunk(spots, slot, rows, piece, student, bias, target, cols, state=(vec, div, grad))
    if groups:
        shift, start, size, _ = pieces[late[-1]]

        def first_row(me=None):
            return source(lax.axis_index("voc") if me is None else me, shift) * padded + start

        def first_id():
            me = lax.axis_index("voc")
            return (source(me, shift) * voc_count + me) * block_cols + start

        step = bias.shape[-1]
        row = first_row(voc_index)
        rows = lax.dynamic_slice(student, (row, 0), (size, tok_rows))
        lines = lax.dynamic_slice(bias, (row // step, 0, 0), (size // step,) + bias.shape[1:])
        operands = [arrived[late[-1]], rows, lines, vec, target]
        limit = block_cols - start if split else None
        div = jnp.sum(div[:8] - vec[2:3] * div[8:], axis=0, keepdims=True) + vec[3:4]
        div = run_tail_sum(operands + [div], first_id, limit)
        grad = run_tail_grad(operands, grad, first_id, first_row, limit)
    else:
        div = jnp.sum(div[:8] - vec[2:3] * div[8:], axis=0, keepdims=True) + vec[3:4]
    loss = div
    for shift in range(1, voc_count):
        loss = loss + swap(div, shift)
    gradient = grad.reshape(voc_count, padded, tok_rows)[:, :block_cols].reshape(vocab_cols, tok_rows).T
    return (gradient, loss.reshape(tok_rows))


def solution(mesh):
    placed = (P("tok", "voc"), P("tok", "voc"), P("tok"), P())

    step = jax.shard_map(body, mesh=mesh, in_specs=placed, out_specs=(P("tok", "voc"), P("tok")), check_vma=False)

    def whole(teacher_logits, student_logits, target_ids, vocab_used):
        run = step
        return run(teacher_logits, student_logits, target_ids, vocab_used)

    return whole
```

```python
import functools

import jax
import jax.numpy as jnp
import numpy as np
from jax import lax
from jax.experimental import pallas as pl
from jax.experimental.pallas import tpu as pltpu
from jax.sharding import PartitionSpec as P

NEG = -1e30
LOW = -3e38
ROWS = 16
LINES = 8
HELD_BYTES = 2.3 * 2**20
WAYS = 3
AHEAD = 1
STEP = 544
LN2 = 0.6931471805599453
F32 = jnp.float32
BF16 = jnp.bfloat16


def largest_part(total, limit):
    best = ROWS
    for size in range(ROWS, limit + 1, ROWS):
        if total % size == 0:
            best = size
    return best


def fold(op, value, height=8):
    return op(value.reshape(-1, height, value.shape[-1]), axis=0)


def addend_rows(rows, masks, pieces):
    parts = []
    for row, mask in zip(rows, masks):
        left = -row
        part = [jnp.ones_like(row) if k == mask else jnp.zeros_like(row) for k in range(2)]
        for _ in range(pieces):
            piece = left.astype(BF16).astype(F32)
            part.append(piece)
            left = left - piece
        part.append(jnp.zeros((LINES - 2 - pieces, row.shape[1]), F32))
        parts.append(jnp.concatenate(part, axis=0))
    return jnp.concatenate(parts, axis=1).astype(BF16)


def addend(mask_ref, n, weights):
    return lax.dot_general(mask_ref[n], weights, (((0,), (0,)), ((), ())), preferred_element_type=F32)


def wide_rows(line, height):
    return jnp.broadcast_to(line, (height, line.shape[-1]))


def stats_kernel(t_ref, s_ref, m_ref, o_ref, tops, sums, block, *, step):
    g = pl.program_id(0)
    rows, lanes = t_ref.shape
    steps = rows // step
    tiles = step // ROWS

    @pl.when(g == 0)
    def _():
        tops[...] = jnp.full(tops.shape, LOW, F32)
        sums[...] = jnp.zeros(sums.shape, F32)

    def part(n):
        return pl.ds(pl.multiple_of(n * step, step), step)

    def first(n, carry):
        tops = list(carry)
        for k in range(tiles):
            tile = pl.ds(pl.multiple_of(n * step + k * ROWS, ROWS), ROWS)
            at = k % WAYS
            tops[at] = jnp.maximum(tops[at], t_ref[tile, :].astype(F32))
            tops[WAYS + at] = jnp.maximum(tops[WAYS + at], s_ref[tile, :].astype(F32))
        return tuple(tops)

    low = jnp.full((ROWS, lanes), LOW, F32)
    highs = lax.fori_loop(0, steps, first, (low,) * (2 * WAYS), unroll=True)
    t_top, s_top = [
        jnp.max(functools.reduce(jnp.maximum, highs[k:k + WAYS]), axis=0, keepdims=True)
        for k in (0, WAYS)]
    weights = addend_rows([t_top, s_top], [0, 1], 1)

    def second(n, carry):
        both = addend(m_ref, n, weights)
        t = t_ref[part(n), :].astype(F32) + both[:, :lanes]
        s = s_ref[part(n), :].astype(F32) + both[:, lanes:]
        return (carry[0] + fold(jnp.sum, jnp.exp(t)), carry[1] + fold(jnp.sum, jnp.exp(s)))

    zero = jnp.zeros((8, lanes), F32)
    t_sum, s_sum = [
        jnp.sum(total, axis=0, keepdims=True)
        for total in lax.fori_loop(0, steps, second, (zero, zero), unroll=True)]
    block[0:1, :] = t_top
    block[1:2, :] = t_sum
    block[2:3, :] = s_top
    block[3:4, :] = s_sum

    @pl.when(jnp.min(jnp.minimum(t_sum, s_sum)) < 1e-10)
    def _():
        blank = jnp.zeros((1, lanes), F32)
        plain = addend_rows([blank, blank], [0, 1], 1)

        def masked(n):
            both = addend(m_ref, n, plain)
            return (
                t_ref[part(n), :].astype(F32) + both[:, :lanes],
                s_ref[part(n), :].astype(F32) + both[:, lanes:])

        def high(n, carry):
            return tuple(jnp.maximum(top, fold(jnp.max, value)) for top, value in zip(carry, masked(n)))

        low = jnp.full((8, lanes), LOW, F32)
        tops = [jnp.max(top, axis=0, keepdims=True) for top in lax.fori_loop(0, steps, high, (low, low))]

        def gather(n, carry):
            return tuple(
                total + fold(jnp.sum, jnp.exp(value - wide_rows(top, step)))
                for total, value, top in zip(carry, masked(n), tops))

        totals = lax.fori_loop(0, steps, gather, (zero, zero))
        for k in range(2):
            block[2 * k:2 * k + 1, :] = tops[k]
            block[2 * k + 1:2 * k + 2, :] = jnp.sum(totals[k], axis=0, keepdims=True)

    for k in range(2):
        old = tops[k:k + 1, :]
        top = block[2 * k:2 * k + 1, :]
        new = jnp.maximum(old, top)
        sums[k:k + 1, :] = (
            sums[k:k + 1, :] * jnp.exp(old - new) + block[2 * k + 1:2 * k + 2, :] * jnp.exp(top - new))
        tops[k:k + 1, :] = new

    @pl.when(g == pl.num_programs(0) - 1)
    def _():
        o_ref[...] = jnp.concatenate(
            [tops[0:1, :], sums[0:1, :], tops[1:2, :], sums[1:2, :], jnp.zeros((4, lanes), F32)], axis=0)


def run_stats(teacher, student, mask, limit):
    total, lanes = teacher.shape
    rows = largest_part(total, limit)
    count = total // rows
    near = pl.BlockSpec((rows, lanes), lambda g: (g, 0))
    step = mask.shape[-1]
    lines = (rows // step,) + mask.shape[1:]
    held = pl.BlockSpec(lines, lambda g: (g, 0, 0))

    def kernel(*refs):
        stats_kernel(*refs, step=step)

    return pl.pallas_call(
        kernel,
        out_shape=jax.ShapeDtypeStruct((8, lanes), F32),
        grid=(count,),
        in_specs=[near, near, held],
        out_specs=pl.BlockSpec((8, lanes), lambda g: (0, 0)),
        scratch_shapes=[pltpu.VMEM((8, lanes), F32)] * 3,
        compiler_params=pltpu.CompilerParams(dimension_semantics=("arbitrary",)),
        name="stats",
    )(teacher, student, mask)


def join_stats(refs, target, tokens):
    parts = [ref[...] for ref in refs]
    t_top = parts[0][0:1]
    s_top = parts[0][2:3]
    kept = parts[0][4:5]
    for part in parts[1:]:
        t_top = jnp.maximum(t_top, part[0:1])
        s_top = jnp.maximum(s_top, part[2:3])
        kept = kept + part[4:5]
    t_sum = jnp.zeros_like(t_top)
    s_sum = jnp.zeros_like(t_top)
    for part in parts:
        t_sum = t_sum + part[1:2] * jnp.exp(part[0:1] - t_top)
        s_sum = s_sum + part[3:4] * jnp.exp(part[2:3] - s_top)
    t_lse = t_top + jnp.log(t_sum)
    s_lse = s_top + jnp.log(s_sum)
    count = jnp.sum(kept, axis=1, keepdims=True)
    weight = jnp.where(target >= 0, (0.5 * tokens) / count, 0.0)
    base = (0.5 * (s_lse - t_lse) + weight * s_lse) * (1.0 / len(parts))
    blank = jnp.zeros((4, target.shape[1]), F32)
    return jnp.concatenate([t_lse + LN2, s_lse - jnp.log(0.5 + weight), weight, base, blank], axis=0)


def chunk_kernel(spots, *refs, spans, slot, step, cols, shares, tokens):
    pieces, refs = refs[:len(spans)], refs[len(spans):]
    s_ref, b_ref, tgt_ref = refs[:3]
    refs = refs[3:]
    g = pl.program_id(0)
    rows, lanes = s_ref.shape
    weights_ref, refs = refs[-1], refs[:-1]
    if shares:
        share_refs, (g_ref, d_out, vec_ref) = refs[:shares], refs[shares:]

        @pl.when(g == 0)
        def _():
            vec_ref[...] = join_stats(share_refs, tgt_ref[...], tokens)
            d_out[...] = jnp.zeros(d_out.shape, F32)
    else:
        vec_ref, d_in, _, g_ref, d_out = refs

        @pl.when(g == 0)
        def _():
            d_out[...] = d_in[...]

    @pl.when(g == 0)
    def _():
        weights_ref[...] = addend_rows([vec_ref[0:1, :], vec_ref[1:2, :]], [1, 1], 3)

    at = 3 * (slot + g)
    base = spots[at + 1]
    away = wide_rows(tgt_ref[...], 8) - lax.broadcasted_iota(jnp.int32, (8, lanes), 0)
    tile = lax.broadcasted_iota(jnp.int32, (step // 8, 8, lanes), 0)
    weight = wide_rows(vec_ref[2:3, :], step)
    weights = weights_ref[...]

    def run(t_ref, first=0):
        def body(n, carry):
            div, picked = carry
            r = pl.multiple_of(n * step, step)
            both = addend(b_ref, n, weights)
            t = t_ref[pl.ds(first + r, step), :].astype(F32)
            s = s_ref[pl.ds(r, step), :].astype(F32)
            tp = jnp.exp(t + both[:, :lanes])
            sp = jnp.exp(s + both[:, lanes:])
            gap = away - (base + r)
            line = jnp.where((gap & 7) == 0, gap >> 3, -1)
            hit = (tile == line[None]).reshape(step, lanes)
            if cols is not None:
                hit = hit & (lax.broadcasted_iota(jnp.int32, (step, lanes), 0) + (spots[at + 2] + r) < cols)
            grad = (sp - tp) - jnp.where(hit, weight, 0.0)
            g_ref[pl.ds(r, step), :] = grad.astype(BF16)
            div = div + fold(jnp.sum, tp * (t - s))
            picked = picked + fold(jnp.sum, jnp.where(hit, s, 0.0))
            return (div, picked)

        div, picked = lax.fori_loop(0, rows // step, body, (d_out[0:8, :], d_out[8:16, :]), unroll=True)
        d_out[0:8, :] = div
        d_out[8:16, :] = picked

    done = 0
    for ref, (length, held) in zip(pieces, spans):
        first = pl.multiple_of((g - done) * rows, rows) if held else 0
        if len(pieces) == 1:
            run(ref, first)
        else:
            pl.when((g >= done) & (g < done + length))(functools.partial(run, ref, first))
        done += length


def run_chunk(spots, slot, rows, pieces, student, bias, target, cols, stats=(), tokens=0, state=None):
    _, lanes = student.shape
    step = bias.shape[-1]
    lines = (rows // step,) + bias.shape[1:]
    spans = [(length, local is None) for _, length, local in pieces]
    moved = pl.BlockSpec((rows, lanes), lambda g, pref: (pref[3 * (slot + g)], 0))
    after = pl.BlockSpec(lines, lambda g, pref: (pref[3 * (slot + g)], 0, 0))

    def fixed(height):
        return pl.BlockSpec((height, lanes), lambda g, pref: (0, 0))

    in_specs, operands = [], [spots]
    done = 0
    for array, length, local in pieces:
        def where(g, pref, done=done, length=length, local=local):
            mine = jnp.clip(g - done, 0, length - 1)
            return ((pref[3 * (slot + done + mine)] if local else mine), 0)

        if local is None:
            in_specs.append(pl.BlockSpec(memory_space=pltpu.VMEM))
            array = pltpu.with_memory_space_constraint(array, pltpu.VMEM)
        else:
            in_specs.append(pl.BlockSpec((rows, lanes), where))
        operands.append(array)
        done += length
    in_specs += [moved, after, fixed(1)]
    operands += [student, bias, target]
    out_shape = [jax.ShapeDtypeStruct(student.shape, BF16)]
    out_specs = [moved]
    aliases = {}
    if stats:
        in_specs += [fixed(8)] * len(stats)
        operands += list(stats)
        out_shape += [jax.ShapeDtypeStruct((16, lanes), F32), jax.ShapeDtypeStruct((8, lanes), F32)]
        out_specs += [fixed(16), fixed(8)]
    else:
        vec, div, grad = state
        in_specs += [fixed(8), fixed(16), pl.BlockSpec(memory_space=pl.ANY)]
        operands += [vec, div, grad]
        aliases = {len(operands) - 1: 0}
        out_shape.append(jax.ShapeDtypeStruct((16, lanes), F32))
        out_specs.append(fixed(16))
    scratch = [pltpu.VMEM((LINES, 2 * lanes), BF16)]

    def kernel(*refs):
        chunk_kernel(*refs, spans=spans, slot=slot, step=step, cols=cols, shares=len(stats), tokens=tokens)

    return pl.pallas_call(
        kernel,
        out_shape=tuple(out_shape),
        grid_spec=pltpu.PrefetchScalarGridSpec(
            num_scalar_prefetch=1,
            grid=(sum(length for length, _ in spans),),
            in_specs=in_specs,
            out_specs=tuple(out_specs),
            scratch_shapes=scratch,
        ),
        input_output_aliases=aliases,
        compiler_params=pltpu.CompilerParams(dimension_semantics=("arbitrary",)),
        name="chunk",
    )(*operands)


def hits(base, r, tgt_ref, step, lanes, limit):
    gap = wide_rows(tgt_ref[...], 8) - lax.broadcasted_iota(jnp.int32, (8, lanes), 0) - (base + r)
    line = jnp.where((gap & 7) == 0, gap >> 3, -1)
    tile = lax.broadcasted_iota(jnp.int32, (step // 8, 8, lanes), 0)
    hit = (tile == line[None]).reshape(step, lanes)
    if limit is not None:
        hit = hit & (lax.broadcasted_iota(jnp.int32, (step, lanes), 0) < limit - r)
    return hit


def tail_sum_kernel(t_ref, s_ref, m_ref, vec_ref, tgt_ref, d_ref, o_ref, *, first_id, limit):
    rows, lanes = t_ref.shape
    step = m_ref.shape[-1]
    weights = addend_rows([vec_ref[0:1, :]], [1], 3)
    base = first_id()
    div = jnp.zeros((8, lanes), F32)
    picked = jnp.zeros((8, lanes), F32)
    for n in range(rows // step):
        t = t_ref[n * step:(n + 1) * step, :].astype(F32)
        s = s_ref[n * step:(n + 1) * step, :].astype(F32)
        tp = jnp.exp(t + addend(m_ref, n, weights))
        div = div + fold(jnp.sum, tp * (t - s))
        hit = hits(base, n * step, tgt_ref, step, lanes, limit)
        picked = picked + fold(jnp.sum, jnp.where(hit, s, 0.0))
    total = div - wide_rows(vec_ref[2:3, :], 8) * picked
    o_ref[...] = jnp.sum(total, axis=0, keepdims=True) + d_ref[...]


def tail_grad_kernel(t_ref, s_ref, m_ref, vec_ref, tgt_ref, _, g_ref, out, sems, *, first_id, first_row, limit):
    rows, lanes = t_ref.shape
    step = m_ref.shape[-1]
    weights = addend_rows([vec_ref[0:1, :], vec_ref[1:2, :]], [1, 1], 3)
    weight = wide_rows(vec_ref[2:3, :], step)
    base = first_id()
    row = first_row()
    copies = []
    for n in range(rows // step):
        part = pl.ds(n * step, step)
        both = addend(m_ref, n, weights)
        tp = jnp.exp(t_ref[part, :].astype(F32) + both[:, :lanes])
        sp = jnp.exp(s_ref[part, :].astype(F32) + both[:, lanes:])
        hit = hits(base, n * step, tgt_ref, step, lanes, limit)
        out[part, :] = ((sp - tp) - jnp.where(hit, weight, 0.0)).astype(BF16)
        place = pl.ds(pl.multiple_of(row + n * step, ROWS), step)
        copies.append(pltpu.make_async_copy(out.at[part, :], g_ref.at[place, :], sems.at[n]))
        copies[-1].start()
    for copy in copies:
        copy.wait()


def held(value):
    return pltpu.with_memory_space_constraint(value, pltpu.VMEM)


def run_tail_sum(operands, first_id, limit):
    lanes = operands[0].shape[1]

    def kernel(*refs):
        tail_sum_kernel(*refs, first_id=first_id, limit=limit)

    return pl.pallas_call(
        kernel,
        out_shape=pltpu.VMEM((1, lanes), F32),
        in_specs=[pl.BlockSpec(memory_space=pltpu.VMEM)] * len(operands),
        out_specs=pl.BlockSpec(memory_space=pltpu.VMEM),
        name="tail_sum",
    )(*[held(value) for value in operands])


def run_tail_grad(operands, grad, first_id, first_row, limit):
    rows, lanes = operands[0].shape
    step = operands[2].shape[-1]

    def kernel(*refs):
        tail_grad_kernel(*refs, first_id=first_id, first_row=first_row, limit=limit)

    return pl.pallas_call(
        kernel,
        out_shape=jax.ShapeDtypeStruct(grad.shape, grad.dtype),
        in_specs=[pl.BlockSpec(memory_space=pltpu.VMEM)] * len(operands) + [pl.BlockSpec(memory_space=pl.ANY)],
        out_specs=pl.BlockSpec(memory_space=pl.ANY),
        scratch_shapes=[pltpu.VMEM((rows, lanes), BF16), pltpu.SemaphoreType.DMA((rows // step,))],
        input_output_aliases={len(operands): 0},
        name="tail_grad",
    )(*[held(value) for value in operands], grad)


def cut_kernel(t_ref, *rest, parts, held, partner):
    outs, rest = rest[:len(parts)], rest[len(parts):]
    stops = outs if held else rest[:len(parts)]
    sems = rest[-1]
    reads, writes = [], []
    me = lax.axis_index("voc")
    for k, (shift, start, size) in enumerate(parts):
        block = partner(me, shift)
        reads.append(pltpu.make_async_copy(t_ref.at[block, pl.ds(start, size), :], stops[k], sems.at[k]))
        reads[-1].start()
    for k in range(len(parts)):
        reads[k].wait()
        if not held:
            writes.append(pltpu.make_async_copy(stops[k], outs[k], sems.at[len(parts) + k]))
            writes[-1].start()
    for copy in writes:
        copy.wait()


def cut(teacher, parts, held, partner):
    lanes = teacher.shape[-1]
    space = pltpu.VMEM if held else pl.ANY
    scratch = [] if held else [pltpu.VMEM((size, lanes), BF16) for _, _, size in parts]

    def kernel(*refs):
        cut_kernel(*refs, parts=parts, held=held, partner=partner)

    return pl.pallas_call(
        kernel,
        out_shape=tuple(
            pltpu.VMEM((size, lanes), BF16) if held else jax.ShapeDtypeStruct((size, lanes), BF16)
            for _, _, size in parts),
        in_specs=[pl.BlockSpec(memory_space=pl.ANY)],
        out_specs=tuple(pl.BlockSpec(memory_space=space) for _ in parts),
        scratch_shapes=scratch + [pltpu.SemaphoreType.DMA((2 * len(parts),))],
        name="cut",
    )(teacher)


def plan(padded, voc_count):
    shifts = list(range(voc_count - 1, 0, -1))
    far = shifts[:-1] if len(shifts) > 1 else shifts
    near = shifts[len(far):]
    big = largest_part(padded, 1600)
    small = largest_part(padded, 544)
    chunked = padded == 3 * big and big == 3 * small
    pieces = []
    for index, shift in enumerate(far):
        if chunked and index == 0:
            pieces += [(shift, 0, big, big), (shift, big, 2 * big, big)]
        elif chunked and index == len(far) - 1:
            pieces += [(shift, 0, AHEAD * small, small), (shift, AHEAD * small, (6 - AHEAD) * small, small),
                       (shift, 2 * big, big, big)]
        else:
            pieces.append((shift, 0, padded, big))
    late = [k for k, piece in enumerate(pieces) if len(far) > 1 and piece[0] == far[-1] and (piece[1] or not chunked)]
    pieces += [(shift, 0, padded, big) for shift in near]
    early = [k for k in range(len(pieces)) if k not in late]
    return pieces, early, late, big


def body(teacher_logits, student_logits, target_ids, vocab_used):
    tok_rows, vocab_cols = teacher_logits.shape
    voc_count = lax.axis_size("voc")
    voc_index = lax.axis_index("voc")
    tok_count = lax.axis_size("tok")
    block_cols = vocab_cols // voc_count
    padded = -(-block_cols // ROWS) * ROWS
    split = padded != block_cols
    paired = voc_count & (voc_count - 1) == 0

    def partner(index, shift):
        return index ^ shift if paired else (index + shift) % voc_count

    def source(index, shift):
        return index ^ shift if paired else (index - shift) % voc_count

    def swap(value, shift):
        return lax.ppermute(value, "voc", [(i, partner(i, shift)) for i in range(voc_count)])

    def blocked(matrix):
        shaped = matrix.T.reshape(voc_count, block_cols, tok_rows)
        if split:
            shaped = jnp.pad(shaped, ((0, 0), (0, padded - block_cols), (0, 0)))
        return shaped

    teacher = blocked(teacher_logits)
    flat = teacher.reshape(voc_count * padded, tok_rows)
    student = blocked(student_logits).reshape(voc_count * padded, tok_rows)
    pieces, early, late, big = plan(padded, voc_count)

    cuts = [piece[:3] for piece in pieces]
    parts = list(cut(teacher, cuts[:1], True, partner))
    parts += list(cut(teacher, cuts[1:], False, partner))
    arrived = []
    for k, piece in enumerate(pieces):
        arrived.append(swap(parts[k], piece[0]))

    target = target_ids.reshape(1, tok_rows)
    kept = (target >= 0).astype(F32)
    merged = 1
    step = 0
    while tok_count // merged > voc_count:
        pairs = [(i, i ^ merged) for i in range(tok_count)]
        if step == 0:
            kept = kept + (lax.ppermute(target, "tok", pairs) >= 0).astype(F32)
        else:
            kept = kept + lax.ppermute(kept, "tok", pairs)
        merged *= 2
        step += 1
    left = tok_count // merged
    even = left & (left - 1) == 0
    pairs = [
        (t * voc_count + v,
         ((t // merged ^ v if even else (t // merged + v) % left) * merged + t % merged) * voc_count + v)
        for t in range(tok_count) for v in range(left)
    ]
    kept = lax.ppermute(kept, ("tok", "voc"), pairs)

    flags = vocab_used.reshape(voc_count, voc_count, block_cols)
    flags = jnp.stack([
        lax.dynamic_index_in_dim(flags, voc_index, 0, keepdims=False),
        lax.dynamic_index_in_dim(flags, voc_index, 1, keepdims=False),
    ])
    line = jnp.where(flags == 1, 0.0, NEG).astype(BF16).reshape(2 * voc_count, block_cols)
    if split:
        line = jnp.pad(line, ((0, 0), (0, padded - block_cols)), constant_values=NEG)
    step = largest_part(padded, STEP)
    line = line.reshape(2, voc_count * padded // step, 1, step)
    kind = lax.broadcasted_iota(jnp.int32, (1, LINES, 1), 1)
    ones = jnp.where(kind < 5, 1.0, 0.0).astype(BF16)
    bias = jnp.where(kind == 0, line[0], jnp.where(kind == 1, line[1], ones))

    stats = run_stats(flat, student, bias, 1600)
    stats = jnp.where(lax.broadcasted_iota(jnp.int32, stats.shape, 0) == 4, kept, stats)
    gathered = [stats]
    for shift in range(1, voc_count):
        gathered.append(swap(stats, shift))

    shift_of, scale, own, fixed = [], [], [], []

    def note(shift, start, size, rows):
        for at in range(start, start + size, rows):
            shift_of.extend([shift] * 3)
            scale.extend([padded // rows, voc_count * block_cols, 0])
            own.extend([0, block_cols, 0])
            fixed.extend([at // rows, at, at])
        return size // rows

    groups = []
    held = [pair[1] for pair in sorted((piece[2], k) for k, piece in enumerate(pieces))]
    held = late + [k for k in reversed(held) if k in early]
    size = 0
    for n, k in enumerate(held):
        size += pieces[k][2] * tok_rows * 2
        if size > HELD_BYTES:
            held = held[:n]
            break
    first = [(flat, note(0, 0, padded, big), True)]
    for k in sorted(early, key=lambda k: k < len(pieces) - 1):
        if pieces[k][3] == big:
            first.append((arrived[k], note(*pieces[k]), None if k in held else False))
    used = sum(length for _, length, _ in first)
    apart = [k for k in early if pieces[k][3] != big]
    for k in late:
        group = []
        start = used
        for j in apart + [k]:
            group.append((arrived[j], note(*pieces[j]), None if j in held else False))
            used += group[-1][1]
        groups.append((start, pieces[k][3], group))
        apart = []
    blocks = source(voc_index, np.array(shift_of, np.int32))
    spots = blocks * np.array(scale, np.int32) + voc_index * np.array(own, np.int32) + np.array(fixed, np.int32)
    spots = spots.astype(jnp.int32)

    cols = block_cols if split else None
    grad, div, vec = run_chunk(
        spots, 0, big, first, student, bias, target, cols, stats=gathered, tokens=tok_rows * tok_count)
    for slot, rows, piece in groups[:-1]:
        grad, div = run_chunk(spots, slot, rows, piece, student, bias, target, cols, state=(vec, div, grad))
    if groups:
        shift, start, size, _ = pieces[late[-1]]

        def first_row(me=None):
            return source(lax.axis_index("voc") if me is None else me, shift) * padded + start

        def first_id():
            me = lax.axis_index("voc")
            return (source(me, shift) * voc_count + me) * block_cols + start

        step = bias.shape[-1]
        row = first_row(voc_index)
        rows = lax.dynamic_slice(student, (row, 0), (size, tok_rows))
        lines = lax.dynamic_slice(bias, (row // step, 0, 0), (size // step,) + bias.shape[1:])
        operands = [arrived[late[-1]], rows, lines, vec, target]
        limit = block_cols - start if split else None
        div = jnp.sum(div[:8] - vec[2:3] * div[8:], axis=0, keepdims=True) + vec[3:4]
        div = run_tail_sum(operands + [div], first_id, limit)
        grad = run_tail_grad(operands, grad, first_id, first_row, limit)
    else:
        div = jnp.sum(div[:8] - vec[2:3] * div[8:], axis=0, keepdims=True) + vec[3:4]
    loss = div
    for shift in range(1, voc_count):
        loss = loss + swap(div, shift)
    gradient = grad.reshape(voc_count, padded, tok_rows)[:, :block_cols].reshape(vocab_cols, tok_rows).T
    return (gradient, loss.reshape(tok_rows))


def solution(mesh):
    placed = (P("tok", "voc"), P("tok", "voc"), P("tok"), P())

    step = jax.shard_map(body, mesh=mesh, in_specs=placed, out_specs=(P("tok", "voc"), P("tok")), check_vma=False)

    def whole(teacher_logits, student_logits, target_ids, vocab_used):
        run = step
        return run(teacher_logits, student_logits, target_ids, vocab_used)

    return whole
```

```python
import functools

import jax
import jax.numpy as jnp
import numpy as np
from jax import lax
from jax.experimental import pallas as pl
from jax.experimental.pallas import tpu as pltpu
from jax.sharding import PartitionSpec as P

NEG = -1e30
LOW = -3e38
ROWS = 16
LINES = 8
HELD_BYTES = 2.3 * 2**20
WAYS = 3
AHEAD = 1
STEP = 544
LN2 = 0.6931471805599453
F32 = jnp.float32
BF16 = jnp.bfloat16


def largest_part(total, limit):
    best = ROWS
    for size in range(ROWS, limit + 1, ROWS):
        if total % size == 0:
            best = size
    return best


def fold(op, value, height=8):
    return op(value.reshape(-1, height, value.shape[-1]), axis=0)


def addend_rows(rows, masks, pieces):
    parts = []
    for row, mask in zip(rows, masks):
        left = -row
        part = [jnp.ones_like(row) if k == mask else jnp.zeros_like(row) for k in range(2)]
        for _ in range(pieces):
            piece = left.astype(BF16).astype(F32)
            part.append(piece)
            left = left - piece
        part.append(jnp.zeros((LINES - 2 - pieces, row.shape[1]), F32))
        parts.append(jnp.concatenate(part, axis=0))
    return jnp.concatenate(parts, axis=1).astype(BF16)


def addend(mask_ref, n, weights):
    return lax.dot_general(mask_ref[n], weights, (((0,), (0,)), ((), ())), preferred_element_type=F32)


def wide_rows(line, height):
    return jnp.broadcast_to(line, (height, line.shape[-1]))


def stats_kernel(t_ref, s_ref, m_ref, o_ref, tops, sums, block, *, step):
    g = pl.program_id(0)
    rows, lanes = t_ref.shape
    steps = rows // step
    tiles = step // ROWS

    @pl.when(g == 0)
    def _():
        tops[...] = jnp.full(tops.shape, LOW, F32)
        sums[...] = jnp.zeros(sums.shape, F32)

    def part(n):
        return pl.ds(pl.multiple_of(n * step, step), step)

    def first(n, carry):
        tops = list(carry)
        for k in range(tiles):
            tile = pl.ds(pl.multiple_of(n * step + k * ROWS, ROWS), ROWS)
            at = k % WAYS
            tops[at] = jnp.maximum(tops[at], t_ref[tile, :].astype(F32))
            tops[WAYS + at] = jnp.maximum(tops[WAYS + at], s_ref[tile, :].astype(F32))
        return tuple(tops)

    low = jnp.full((ROWS, lanes), LOW, F32)
    highs = lax.fori_loop(0, steps, first, (low,) * (2 * WAYS), unroll=True)
    t_top, s_top = [
        jnp.max(functools.reduce(jnp.maximum, highs[k:k + WAYS]), axis=0, keepdims=True)
        for k in (0, WAYS)]
    weights = addend_rows([t_top, s_top], [0, 1], 1)

    def second(n, carry):
        both = addend(m_ref, n, weights)
        t = t_ref[part(n), :].astype(F32) + both[:, :lanes]
        s = s_ref[part(n), :].astype(F32) + both[:, lanes:]
        return (carry[0] + fold(jnp.sum, jnp.exp(t)), carry[1] + fold(jnp.sum, jnp.exp(s)))

    zero = jnp.zeros((8, lanes), F32)
    t_sum, s_sum = [
        jnp.sum(total, axis=0, keepdims=True)
        for total in lax.fori_loop(0, steps, second, (zero, zero), unroll=True)]
    block[0:1, :] = t_top
    block[1:2, :] = t_sum
    block[2:3, :] = s_top
    block[3:4, :] = s_sum

    @pl.when(jnp.min(jnp.minimum(t_sum, s_sum)) < 1e-10)
    def _():
        blank = jnp.zeros((1, lanes), F32)
        plain = addend_rows([blank, blank], [0, 1], 1)

        def masked(n):
            both = addend(m_ref, n, plain)
            return (
                t_ref[part(n), :].astype(F32) + both[:, :lanes],
                s_ref[part(n), :].astype(F32) + both[:, lanes:])

        def high(n, carry):
            return tuple(jnp.maximum(top, fold(jnp.max, value)) for top, value in zip(carry, masked(n)))

        low = jnp.full((8, lanes), LOW, F32)
        tops = [jnp.max(top, axis=0, keepdims=True) for top in lax.fori_loop(0, steps, high, (low, low))]

        def gather(n, carry):
            return tuple(
                total + fold(jnp.sum, jnp.exp(value - wide_rows(top, step)))
                for total, value, top in zip(carry, masked(n), tops))

        totals = lax.fori_loop(0, steps, gather, (zero, zero))
        for k in range(2):
            block[2 * k:2 * k + 1, :] = tops[k]
            block[2 * k + 1:2 * k + 2, :] = jnp.sum(totals[k], axis=0, keepdims=True)

    for k in range(2):
        old = tops[k:k + 1, :]
        top = block[2 * k:2 * k + 1, :]
        new = jnp.maximum(old, top)
        sums[k:k + 1, :] = (
            sums[k:k + 1, :] * jnp.exp(old - new) + block[2 * k + 1:2 * k + 2, :] * jnp.exp(top - new))
        tops[k:k + 1, :] = new

    @pl.when(g == pl.num_programs(0) - 1)
    def _():
        o_ref[...] = jnp.concatenate(
            [tops[0:1, :], sums[0:1, :], tops[1:2, :], sums[1:2, :], jnp.zeros((4, lanes), F32)], axis=0)


def run_stats(teacher, student, mask, limit):
    total, lanes = teacher.shape
    rows = largest_part(total, limit)
    count = total // rows
    near = pl.BlockSpec((rows, lanes), lambda g: (g, 0))
    step = mask.shape[-1]
    lines = (rows // step,) + mask.shape[1:]
    held = pl.BlockSpec(lines, lambda g: (g, 0, 0))

    def kernel(*refs):
        stats_kernel(*refs, step=step)

    return pl.pallas_call(
        kernel,
        out_shape=jax.ShapeDtypeStruct((8, lanes), F32),
        grid=(count,),
        in_specs=[near, near, held],
        out_specs=pl.BlockSpec((8, lanes), lambda g: (0, 0)),
        scratch_shapes=[pltpu.VMEM((8, lanes), F32)] * 3,
        compiler_params=pltpu.CompilerParams(dimension_semantics=("arbitrary",)),
        name="stats",
    )(teacher, student, mask)


def join_stats(refs, kept, target, tokens):
    parts = [ref[...] for ref in refs]
    t_top = parts[0][0:1]
    s_top = parts[0][2:3]
    for part in parts[1:]:
        t_top = jnp.maximum(t_top, part[0:1])
        s_top = jnp.maximum(s_top, part[2:3])
    t_sum = jnp.zeros_like(t_top)
    s_sum = jnp.zeros_like(t_top)
    for part in parts:
        t_sum = t_sum + part[1:2] * jnp.exp(part[0:1] - t_top)
        s_sum = s_sum + part[3:4] * jnp.exp(part[2:3] - s_top)
    t_lse = t_top + jnp.log(t_sum)
    s_lse = s_top + jnp.log(s_sum)
    count = jnp.sum(kept, axis=1, keepdims=True)
    weight = jnp.where(target >= 0, (0.5 * tokens) / count, 0.0)
    base = (0.5 * (s_lse - t_lse) + weight * s_lse) * (1.0 / len(parts))
    blank = jnp.zeros((4, target.shape[1]), F32)
    return jnp.concatenate([t_lse + LN2, s_lse - jnp.log(0.5 + weight), weight, base, blank], axis=0)


def chunk_kernel(spots, *refs, spans, slot, step, cols, shares, tokens):
    pieces, refs = refs[:len(spans)], refs[len(spans):]
    s_ref, b_ref, tgt_ref = refs[:3]
    refs = refs[3:]
    g = pl.program_id(0)
    rows, lanes = s_ref.shape
    weights_ref, refs = refs[-1], refs[:-1]
    if shares:
        share_refs, (kept_ref, g_ref, d_out, vec_ref) = refs[:shares], refs[shares:]

        @pl.when(g == 0)
        def _():
            vec_ref[...] = join_stats(share_refs, kept_ref[...], tgt_ref[...], tokens)
            d_out[...] = jnp.zeros(d_out.shape, F32)
    else:
        vec_ref, d_in, _, g_ref, d_out = refs

        @pl.when(g == 0)
        def _():
            d_out[...] = d_in[...]

    @pl.when(g == 0)
    def _():
        weights_ref[...] = addend_rows([vec_ref[0:1, :], vec_ref[1:2, :]], [1, 1], 3)

    at = 3 * (slot + g)
    base = spots[at + 1]
    away = wide_rows(tgt_ref[...], 8) - lax.broadcasted_iota(jnp.int32, (8, lanes), 0)
    tile = lax.broadcasted_iota(jnp.int32, (step // 8, 8, lanes), 0)
    weight = wide_rows(vec_ref[2:3, :], step)
    weights = weights_ref[...]

    def run(t_ref, first=0):
        def body(n, carry):
            div, picked = carry
            r = pl.multiple_of(n * step, step)
            both = addend(b_ref, n, weights)
            t = t_ref[pl.ds(first + r, step), :].astype(F32)
            s = s_ref[pl.ds(r, step), :].astype(F32)
            tp = jnp.exp(t + both[:, :lanes])
            sp = jnp.exp(s + both[:, lanes:])
            gap = away - (base + r)
            line = jnp.where((gap & 7) == 0, gap >> 3, -1)
            hit = (tile == line[None]).reshape(step, lanes)
            if cols is not None:
                hit = hit & (lax.broadcasted_iota(jnp.int32, (step, lanes), 0) + (spots[at + 2] + r) < cols)
            grad = (sp - tp) - jnp.where(hit, weight, 0.0)
            g_ref[pl.ds(r, step), :] = grad.astype(BF16)
            div = div + fold(jnp.sum, tp * (t - s))
            picked = picked + fold(jnp.sum, jnp.where(hit, s, 0.0))
            return (div, picked)

        div, picked = lax.fori_loop(0, rows // step, body, (d_out[0:8, :], d_out[8:16, :]), unroll=True)
        d_out[0:8, :] = div
        d_out[8:16, :] = picked

    done = 0
    for ref, (length, held) in zip(pieces, spans):
        first = pl.multiple_of((g - done) * rows, rows) if held else 0
        if len(pieces) == 1:
            run(ref, first)
        else:
            pl.when((g >= done) & (g < done + length))(functools.partial(run, ref, first))
        done += length


def run_chunk(spots, slot, rows, pieces, student, bias, target, cols, stats=(), kept=None, tokens=0, state=None):
    _, lanes = student.shape
    step = bias.shape[-1]
    lines = (rows // step,) + bias.shape[1:]
    spans = [(length, local is None) for _, length, local in pieces]
    moved = pl.BlockSpec((rows, lanes), lambda g, pref: (pref[3 * (slot + g)], 0))
    after = pl.BlockSpec(lines, lambda g, pref: (pref[3 * (slot + g)], 0, 0))

    def fixed(height):
        return pl.BlockSpec((height, lanes), lambda g, pref: (0, 0))

    in_specs, operands = [], [spots]
    done = 0
    for array, length, local in pieces:
        def where(g, pref, done=done, length=length, local=local):
            mine = jnp.clip(g - done, 0, length - 1)
            return ((pref[3 * (slot + done + mine)] if local else mine), 0)

        if local is None:
            in_specs.append(pl.BlockSpec(memory_space=pltpu.VMEM))
            array = pltpu.with_memory_space_constraint(array, pltpu.VMEM)
        else:
            in_specs.append(pl.BlockSpec((rows, lanes), where))
        operands.append(array)
        done += length
    in_specs += [moved, after, fixed(1)]
    operands += [student, bias, target]
    out_shape = [jax.ShapeDtypeStruct(student.shape, BF16)]
    out_specs = [moved]
    aliases = {}
    if stats:
        in_specs += [fixed(8)] * len(stats) + [fixed(1)]
        operands += list(stats) + [kept]
        out_shape += [jax.ShapeDtypeStruct((16, lanes), F32), jax.ShapeDtypeStruct((8, lanes), F32)]
        out_specs += [fixed(16), fixed(8)]
    else:
        vec, div, grad = state
        in_specs += [fixed(8), fixed(16), pl.BlockSpec(memory_space=pl.ANY)]
        operands += [vec, div, grad]
        aliases = {len(operands) - 1: 0}
        out_shape.append(jax.ShapeDtypeStruct((16, lanes), F32))
        out_specs.append(fixed(16))
    scratch = [pltpu.VMEM((LINES, 2 * lanes), BF16)]

    def kernel(*refs):
        chunk_kernel(*refs, spans=spans, slot=slot, step=step, cols=cols, shares=len(stats), tokens=tokens)

    return pl.pallas_call(
        kernel,
        out_shape=tuple(out_shape),
        grid_spec=pltpu.PrefetchScalarGridSpec(
            num_scalar_prefetch=1,
            grid=(sum(length for length, _ in spans),),
            in_specs=in_specs,
            out_specs=tuple(out_specs),
            scratch_shapes=scratch,
        ),
        input_output_aliases=aliases,
        compiler_params=pltpu.CompilerParams(dimension_semantics=("arbitrary",)),
        name="chunk",
    )(*operands)


def hits(base, r, tgt_ref, step, lanes, limit):
    gap = wide_rows(tgt_ref[...], 8) - lax.broadcasted_iota(jnp.int32, (8, lanes), 0) - (base + r)
    line = jnp.where((gap & 7) == 0, gap >> 3, -1)
    tile = lax.broadcasted_iota(jnp.int32, (step // 8, 8, lanes), 0)
    hit = (tile == line[None]).reshape(step, lanes)
    if limit is not None:
        hit = hit & (lax.broadcasted_iota(jnp.int32, (step, lanes), 0) < limit - r)
    return hit


def tail_sum_kernel(t_ref, s_ref, m_ref, vec_ref, tgt_ref, d_ref, o_ref, *, first_id, limit):
    rows, lanes = t_ref.shape
    step = m_ref.shape[-1]
    weights = addend_rows([vec_ref[0:1, :]], [1], 3)
    base = first_id()
    div = jnp.zeros((8, lanes), F32)
    picked = jnp.zeros((8, lanes), F32)
    for n in range(rows // step):
        t = t_ref[n * step:(n + 1) * step, :].astype(F32)
        s = s_ref[n * step:(n + 1) * step, :].astype(F32)
        tp = jnp.exp(t + addend(m_ref, n, weights))
        div = div + fold(jnp.sum, tp * (t - s))
        hit = hits(base, n * step, tgt_ref, step, lanes, limit)
        picked = picked + fold(jnp.sum, jnp.where(hit, s, 0.0))
    total = div - wide_rows(vec_ref[2:3, :], 8) * picked
    o_ref[...] = jnp.sum(total, axis=0, keepdims=True) + d_ref[...]


def tail_grad_kernel(t_ref, s_ref, m_ref, vec_ref, tgt_ref, _, g_ref, out, sems, *, first_id, first_row, limit):
    rows, lanes = t_ref.shape
    step = m_ref.shape[-1]
    weights = addend_rows([vec_ref[0:1, :], vec_ref[1:2, :]], [1, 1], 3)
    weight = wide_rows(vec_ref[2:3, :], step)
    base = first_id()
    row = first_row()
    copies = []
    for n in range(rows // step):
        part = pl.ds(n * step, step)
        both = addend(m_ref, n, weights)
        tp = jnp.exp(t_ref[part, :].astype(F32) + both[:, :lanes])
        sp = jnp.exp(s_ref[part, :].astype(F32) + both[:, lanes:])
        hit = hits(base, n * step, tgt_ref, step, lanes, limit)
        out[part, :] = ((sp - tp) - jnp.where(hit, weight, 0.0)).astype(BF16)
        place = pl.ds(pl.multiple_of(row + n * step, ROWS), step)
        copies.append(pltpu.make_async_copy(out.at[part, :], g_ref.at[place, :], sems.at[n]))
        copies[-1].start()
    for copy in copies:
        copy.wait()


def held(value):
    return pltpu.with_memory_space_constraint(value, pltpu.VMEM)


def run_tail_sum(operands, first_id, limit):
    lanes = operands[0].shape[1]

    def kernel(*refs):
        tail_sum_kernel(*refs, first_id=first_id, limit=limit)

    return pl.pallas_call(
        kernel,
        out_shape=pltpu.VMEM((1, lanes), F32),
        in_specs=[pl.BlockSpec(memory_space=pltpu.VMEM)] * len(operands),
        out_specs=pl.BlockSpec(memory_space=pltpu.VMEM),
        name="tail_sum",
    )(*[held(value) for value in operands])


def run_tail_grad(operands, grad, first_id, first_row, limit):
    rows, lanes = operands[0].shape
    step = operands[2].shape[-1]

    def kernel(*refs):
        tail_grad_kernel(*refs, first_id=first_id, first_row=first_row, limit=limit)

    return pl.pallas_call(
        kernel,
        out_shape=jax.ShapeDtypeStruct(grad.shape, grad.dtype),
        in_specs=[pl.BlockSpec(memory_space=pltpu.VMEM)] * len(operands) + [pl.BlockSpec(memory_space=pl.ANY)],
        out_specs=pl.BlockSpec(memory_space=pl.ANY),
        scratch_shapes=[pltpu.VMEM((rows, lanes), BF16), pltpu.SemaphoreType.DMA((rows // step,))],
        input_output_aliases={len(operands): 0},
        name="tail_grad",
    )(*[held(value) for value in operands], grad)


def cut_kernel(t_ref, *rest, parts, held, partner):
    outs, rest = rest[:len(parts)], rest[len(parts):]
    stops = outs if held else rest[:len(parts)]
    sems = rest[-1]
    reads, writes = [], []
    me = lax.axis_index("voc")
    for k, (shift, start, size) in enumerate(parts):
        block = partner(me, shift)
        reads.append(pltpu.make_async_copy(t_ref.at[block, pl.ds(start, size), :], stops[k], sems.at[k]))
        reads[-1].start()
    for k in range(len(parts)):
        reads[k].wait()
        if not held:
            writes.append(pltpu.make_async_copy(stops[k], outs[k], sems.at[len(parts) + k]))
            writes[-1].start()
    for copy in writes:
        copy.wait()


def cut(teacher, parts, held, partner):
    lanes = teacher.shape[-1]
    space = pltpu.VMEM if held else pl.ANY
    scratch = [] if held else [pltpu.VMEM((size, lanes), BF16) for _, _, size in parts]

    def kernel(*refs):
        cut_kernel(*refs, parts=parts, held=held, partner=partner)

    return pl.pallas_call(
        kernel,
        out_shape=tuple(
            pltpu.VMEM((size, lanes), BF16) if held else jax.ShapeDtypeStruct((size, lanes), BF16)
            for _, _, size in parts),
        in_specs=[pl.BlockSpec(memory_space=pl.ANY)],
        out_specs=tuple(pl.BlockSpec(memory_space=space) for _ in parts),
        scratch_shapes=scratch + [pltpu.SemaphoreType.DMA((2 * len(parts),))],
        name="cut",
    )(teacher)


def plan(padded, voc_count):
    shifts = list(range(voc_count - 1, 0, -1))
    far = shifts[:-1] if len(shifts) > 1 else shifts
    near = shifts[len(far):]
    big = largest_part(padded, 1600)
    small = largest_part(padded, 544)
    chunked = padded == 3 * big and big == 3 * small
    pieces = []
    for index, shift in enumerate(far):
        if chunked and index == 0:
            pieces += [(shift, 0, big, big), (shift, big, 2 * big, big)]
        elif chunked and index == len(far) - 1:
            pieces += [(shift, 0, AHEAD * small, small), (shift, AHEAD * small, (6 - AHEAD) * small, small),
                       (shift, 2 * big, big, big)]
        else:
            pieces.append((shift, 0, padded, big))
    late = [k for k, piece in enumerate(pieces) if len(far) > 1 and piece[0] == far[-1] and (piece[1] or not chunked)]
    pieces += [(shift, 0, padded, big) for shift in near]
    early = [k for k in range(len(pieces)) if k not in late]
    return pieces, early, late, big


def body(teacher_logits, student_logits, target_ids, vocab_used):
    tok_rows, vocab_cols = teacher_logits.shape
    voc_count = lax.axis_size("voc")
    voc_index = lax.axis_index("voc")
    tok_count = lax.axis_size("tok")
    block_cols = vocab_cols // voc_count
    padded = -(-block_cols // ROWS) * ROWS
    split = padded != block_cols
    paired = voc_count & (voc_count - 1) == 0

    def partner(index, shift):
        return index ^ shift if paired else (index + shift) % voc_count

    def source(index, shift):
        return index ^ shift if paired else (index - shift) % voc_count

    def swap(value, shift):
        return lax.ppermute(value, "voc", [(i, partner(i, shift)) for i in range(voc_count)])

    def blocked(matrix):
        shaped = matrix.T.reshape(voc_count, block_cols, tok_rows)
        if split:
            shaped = jnp.pad(shaped, ((0, 0), (0, padded - block_cols), (0, 0)))
        return shaped

    teacher = blocked(teacher_logits)
    flat = teacher.reshape(voc_count * padded, tok_rows)
    student = blocked(student_logits).reshape(voc_count * padded, tok_rows)
    pieces, early, late, big = plan(padded, voc_count)

    cuts = [piece[:3] for piece in pieces]
    parts = list(cut(teacher, cuts[:1], True, partner))
    parts += list(cut(teacher, cuts[1:], False, partner))
    arrived = []
    for k, piece in enumerate(pieces):
        arrived.append(swap(parts[k], piece[0]))

    target = target_ids.reshape(1, tok_rows)
    kept = (target >= 0).astype(F32)
    if tok_count & (tok_count - 1):
        kept = lax.psum(kept, "tok")
    else:
        for step in range(tok_count.bit_length() - 1):
            pairs = [(i, i ^ 1 << step) for i in range(tok_count)]
            if step == 0:
                kept = kept + (lax.ppermute(target, "tok", pairs) >= 0).astype(F32)
            else:
                kept = kept + lax.ppermute(kept, "tok", pairs)

    flags = vocab_used.reshape(voc_count, voc_count, block_cols)
    flags = jnp.stack([
        lax.dynamic_index_in_dim(flags, voc_index, 0, keepdims=False),
        lax.dynamic_index_in_dim(flags, voc_index, 1, keepdims=False),
    ])
    line = jnp.where(flags == 1, 0.0, NEG).astype(BF16).reshape(2 * voc_count, block_cols)
    if split:
        line = jnp.pad(line, ((0, 0), (0, padded - block_cols)), constant_values=NEG)
    step = largest_part(padded, STEP)
    line = line.reshape(2, voc_count * padded // step, 1, step)
    kind = lax.broadcasted_iota(jnp.int32, (1, LINES, 1), 1)
    ones = jnp.where(kind < 5, 1.0, 0.0).astype(BF16)
    bias = jnp.where(kind == 0, line[0], jnp.where(kind == 1, line[1], ones))

    stats = run_stats(flat, student, bias, 1600)
    gathered = [stats]
    for shift in range(1, voc_count):
        gathered.append(swap(stats, shift))

    shift_of, scale, own, fixed = [], [], [], []

    def note(shift, start, size, rows):
        for at in range(start, start + size, rows):
            shift_of.extend([shift] * 3)
            scale.extend([padded // rows, voc_count * block_cols, 0])
            own.extend([0, block_cols, 0])
            fixed.extend([at // rows, at, at])
        return size // rows

    groups = []
    held = [pair[1] for pair in sorted((piece[2], k) for k, piece in enumerate(pieces))]
    held = late + [k for k in reversed(held) if k in early]
    size = 0
    for n, k in enumerate(held):
        size += pieces[k][2] * tok_rows * 2
        if size > HELD_BYTES:
            held = held[:n]
            break
    first = [(flat, note(0, 0, padded, big), True)]
    for k in sorted(early, key=lambda k: k < len(pieces) - 1):
        if pieces[k][3] == big:
            first.append((arrived[k], note(*pieces[k]), None if k in held else False))
    used = sum(length for _, length, _ in first)
    apart = [k for k in early if pieces[k][3] != big]
    for k in late:
        group = []
        start = used
        for j in apart + [k]:
            group.append((arrived[j], note(*pieces[j]), None if j in held else False))
            used += group[-1][1]
        groups.append((start, pieces[k][3], group))
        apart = []
    blocks = source(voc_index, np.array(shift_of, np.int32))
    spots = blocks * np.array(scale, np.int32) + voc_index * np.array(own, np.int32) + np.array(fixed, np.int32)
    spots = spots.astype(jnp.int32)

    cols = block_cols if split else None
    grad, div, vec = run_chunk(
        spots, 0, big, first, student, bias, target, cols, stats=gathered, kept=kept,
        tokens=tok_rows * tok_count)
    for slot, rows, piece in groups[:-1]:
        grad, div = run_chunk(spots, slot, rows, piece, student, bias, target, cols, state=(vec, div, grad))
    if groups:
        shift, start, size, _ = pieces[late[-1]]

        def first_row(me=None):
            return source(lax.axis_index("voc") if me is None else me, shift) * padded + start

        def first_id():
            me = lax.axis_index("voc")
            return (source(me, shift) * voc_count + me) * block_cols + start

        step = bias.shape[-1]
        row = first_row(voc_index)
        rows = lax.dynamic_slice(student, (row, 0), (size, tok_rows))
        lines = lax.dynamic_slice(bias, (row // step, 0, 0), (size // step,) + bias.shape[1:])
        operands = [arrived[late[-1]], rows, lines, vec, target]
        limit = block_cols - start if split else None
        div = jnp.sum(div[:8] - vec[2:3] * div[8:], axis=0, keepdims=True) + vec[3:4]
        div = run_tail_sum(operands + [div], first_id, limit)
        grad = run_tail_grad(operands, grad, first_id, first_row, limit)
    else:
        div = jnp.sum(div[:8] - vec[2:3] * div[8:], axis=0, keepdims=True) + vec[3:4]
    loss = div
    for shift in range(1, voc_count):
        loss = loss + swap(div, shift)
    gradient = grad.reshape(voc_count, padded, tok_rows)[:, :block_cols].reshape(vocab_cols, tok_rows).T
    return (gradient, loss.reshape(tok_rows))


def solution(mesh):
    placed = (P("tok", "voc"), P("tok", "voc"), P("tok"), P())

    step = jax.shard_map(body, mesh=mesh, in_specs=placed, out_specs=(P("tok", "voc"), P("tok")), check_vma=False)

    def whole(teacher_logits, student_logits, target_ids, vocab_used):
        run = step
        return run(teacher_logits, student_logits, target_ids, vocab_used)

    return whole
```

```python
import functools

import jax
import jax.numpy as jnp
import numpy as np
from jax import lax
from jax.experimental import pallas as pl
from jax.experimental.pallas import tpu as pltpu
from jax.sharding import PartitionSpec as P

NEG = -1e30
LOW = -3e38
ROWS = 16
LINES = 8
HELD_BYTES = 2.4 * 2**20
WAYS = 3
STEP = 544
LN2 = 0.6931471805599453
F32 = jnp.float32
BF16 = jnp.bfloat16


def largest_part(total, limit):
    best = ROWS
    for size in range(ROWS, limit + 1, ROWS):
        if total % size == 0:
            best = size
    return best


def fold(op, value, height=8):
    return op(value.reshape(-1, height, value.shape[-1]), axis=0)


def addend_rows(rows, masks, pieces):
    parts = []
    for row, mask in zip(rows, masks):
        left = -row
        part = [jnp.ones_like(row) if k == mask else jnp.zeros_like(row) for k in range(2)]
        for _ in range(pieces):
            piece = left.astype(BF16).astype(F32)
            part.append(piece)
            left = left - piece
        part.append(jnp.zeros((LINES - 2 - pieces, row.shape[1]), F32))
        parts.append(jnp.concatenate(part, axis=0))
    return jnp.concatenate(parts, axis=1).astype(BF16)


def addend(mask_ref, n, weights):
    return lax.dot_general(mask_ref[n], weights, (((0,), (0,)), ((), ())), preferred_element_type=F32)


def wide_rows(line, height):
    return jnp.broadcast_to(line, (height, line.shape[-1]))


def stats_kernel(t_ref, s_ref, m_ref, o_ref, tops, sums, block, *, step):
    g = pl.program_id(0)
    rows, lanes = t_ref.shape
    steps = rows // step
    tiles = step // ROWS

    @pl.when(g == 0)
    def _():
        tops[...] = jnp.full(tops.shape, LOW, F32)
        sums[...] = jnp.zeros(sums.shape, F32)

    def part(n):
        return pl.ds(pl.multiple_of(n * step, step), step)

    def first(n, carry):
        tops = list(carry)
        for k in range(tiles):
            tile = pl.ds(pl.multiple_of(n * step + k * ROWS, ROWS), ROWS)
            at = k % WAYS
            tops[at] = jnp.maximum(tops[at], t_ref[tile, :].astype(F32))
            tops[WAYS + at] = jnp.maximum(tops[WAYS + at], s_ref[tile, :].astype(F32))
        return tuple(tops)

    low = jnp.full((ROWS, lanes), LOW, F32)
    highs = lax.fori_loop(0, steps, first, (low,) * (2 * WAYS), unroll=True)
    t_top, s_top = [
        jnp.max(functools.reduce(jnp.maximum, highs[k:k + WAYS]), axis=0, keepdims=True)
        for k in (0, WAYS)]
    weights = addend_rows([t_top, s_top], [0, 1], 1)

    def second(n, carry):
        both = addend(m_ref, n, weights)
        t = t_ref[part(n), :].astype(F32) + both[:, :lanes]
        s = s_ref[part(n), :].astype(F32) + both[:, lanes:]
        return (carry[0] + fold(jnp.sum, jnp.exp(t)), carry[1] + fold(jnp.sum, jnp.exp(s)))

    zero = jnp.zeros((8, lanes), F32)
    t_sum, s_sum = [
        jnp.sum(total, axis=0, keepdims=True)
        for total in lax.fori_loop(0, steps, second, (zero, zero), unroll=True)]
    block[0:1, :] = t_top
    block[1:2, :] = t_sum
    block[2:3, :] = s_top
    block[3:4, :] = s_sum

    @pl.when(jnp.min(jnp.minimum(t_sum, s_sum)) < 1e-10)
    def _():
        blank = jnp.zeros((1, lanes), F32)
        plain = addend_rows([blank, blank], [0, 1], 1)

        def masked(n):
            both = addend(m_ref, n, plain)
            return (
                t_ref[part(n), :].astype(F32) + both[:, :lanes],
                s_ref[part(n), :].astype(F32) + both[:, lanes:])

        def high(n, carry):
            return tuple(jnp.maximum(top, fold(jnp.max, value)) for top, value in zip(carry, masked(n)))

        low = jnp.full((8, lanes), LOW, F32)
        tops = [jnp.max(top, axis=0, keepdims=True) for top in lax.fori_loop(0, steps, high, (low, low))]

        def gather(n, carry):
            return tuple(
                total + fold(jnp.sum, jnp.exp(value - wide_rows(top, step)))
                for total, value, top in zip(carry, masked(n), tops))

        totals = lax.fori_loop(0, steps, gather, (zero, zero))
        for k in range(2):
            block[2 * k:2 * k + 1, :] = tops[k]
            block[2 * k + 1:2 * k + 2, :] = jnp.sum(totals[k], axis=0, keepdims=True)

    for k in range(2):
        old = tops[k:k + 1, :]
        top = block[2 * k:2 * k + 1, :]
        new = jnp.maximum(old, top)
        sums[k:k + 1, :] = (
            sums[k:k + 1, :] * jnp.exp(old - new) + block[2 * k + 1:2 * k + 2, :] * jnp.exp(top - new))
        tops[k:k + 1, :] = new

    @pl.when(g == pl.num_programs(0) - 1)
    def _():
        o_ref[...] = jnp.concatenate(
            [tops[0:1, :], sums[0:1, :], tops[1:2, :], sums[1:2, :], jnp.zeros((4, lanes), F32)], axis=0)


def run_stats(teacher, student, mask, limit):
    total, lanes = teacher.shape
    rows = largest_part(total, limit)
    count = total // rows
    near = pl.BlockSpec((rows, lanes), lambda g: (g, 0))
    step = mask.shape[-1]
    lines = (rows // step,) + mask.shape[1:]
    held = pl.BlockSpec(lines, lambda g: (g, 0, 0))

    def kernel(*refs):
        stats_kernel(*refs, step=step)

    return pl.pallas_call(
        kernel,
        out_shape=jax.ShapeDtypeStruct((8, lanes), F32),
        grid=(count,),
        in_specs=[near, near, held],
        out_specs=pl.BlockSpec((8, lanes), lambda g: (0, 0)),
        scratch_shapes=[pltpu.VMEM((8, lanes), F32)] * 3,
        compiler_params=pltpu.CompilerParams(dimension_semantics=("arbitrary",)),
        name="stats",
    )(teacher, student, mask)


def join_stats(refs, kept, target, tokens):
    parts = [ref[...] for ref in refs]
    t_top = parts[0][0:1]
    s_top = parts[0][2:3]
    for part in parts[1:]:
        t_top = jnp.maximum(t_top, part[0:1])
        s_top = jnp.maximum(s_top, part[2:3])
    t_sum = jnp.zeros_like(t_top)
    s_sum = jnp.zeros_like(t_top)
    for part in parts:
        t_sum = t_sum + part[1:2] * jnp.exp(part[0:1] - t_top)
        s_sum = s_sum + part[3:4] * jnp.exp(part[2:3] - s_top)
    t_lse = t_top + jnp.log(t_sum)
    s_lse = s_top + jnp.log(s_sum)
    count = jnp.sum(kept, axis=1, keepdims=True)
    weight = jnp.where(target >= 0, (0.5 * tokens) / count, 0.0)
    base = (0.5 * (s_lse - t_lse) + weight * s_lse) * (1.0 / len(parts))
    blank = jnp.zeros((4, target.shape[1]), F32)
    return jnp.concatenate([t_lse + LN2, s_lse - jnp.log(0.5 + weight), weight, base, blank], axis=0)


def chunk_kernel(spots, *refs, spans, slot, step, cols, shares, tokens):
    pieces, refs = refs[:len(spans)], refs[len(spans):]
    s_ref, b_ref, tgt_ref = refs[:3]
    refs = refs[3:]
    g = pl.program_id(0)
    rows, lanes = s_ref.shape
    weights_ref, refs = refs[-1], refs[:-1]
    if shares:
        share_refs, (kept_ref, g_ref, d_out, vec_ref) = refs[:shares], refs[shares:]

        @pl.when(g == 0)
        def _():
            vec_ref[...] = join_stats(share_refs, kept_ref[...], tgt_ref[...], tokens)
            d_out[...] = jnp.zeros(d_out.shape, F32)
    else:
        vec_ref, d_in, _, g_ref, d_out = refs

        @pl.when(g == 0)
        def _():
            d_out[...] = d_in[...]

    @pl.when(g == 0)
    def _():
        weights_ref[...] = addend_rows([vec_ref[0:1, :], vec_ref[1:2, :]], [1, 1], 3)

    at = 3 * (slot + g)
    base = spots[at + 1]
    away = wide_rows(tgt_ref[...], 8) - lax.broadcasted_iota(jnp.int32, (8, lanes), 0)
    tile = lax.broadcasted_iota(jnp.int32, (step // 8, 8, lanes), 0)
    weight = wide_rows(vec_ref[2:3, :], step)
    weights = weights_ref[...]

    def run(t_ref, first=0):
        def body(n, carry):
            div, picked = carry
            r = pl.multiple_of(n * step, step)
            both = addend(b_ref, n, weights)
            t = t_ref[pl.ds(first + r, step), :].astype(F32)
            s = s_ref[pl.ds(r, step), :].astype(F32)
            tp = jnp.exp(t + both[:, :lanes])
            sp = jnp.exp(s + both[:, lanes:])
            gap = away - (base + r)
            line = jnp.where((gap & 7) == 0, gap >> 3, -1)
            hit = (tile == line[None]).reshape(step, lanes)
            if cols is not None:
                hit = hit & (lax.broadcasted_iota(jnp.int32, (step, lanes), 0) + (spots[at + 2] + r) < cols)
            grad = (sp - tp) - jnp.where(hit, weight, 0.0)
            g_ref[pl.ds(r, step), :] = grad.astype(BF16)
            div = div + fold(jnp.sum, tp * (t - s))
            picked = picked + fold(jnp.sum, jnp.where(hit, s, 0.0))
            return (div, picked)

        div, picked = lax.fori_loop(0, rows // step, body, (d_out[0:8, :], d_out[8:16, :]), unroll=True)
        d_out[0:8, :] = div
        d_out[8:16, :] = picked

    done = 0
    for ref, (length, held) in zip(pieces, spans):
        first = pl.multiple_of((g - done) * rows, rows) if held else 0
        if len(pieces) == 1:
            run(ref, first)
        else:
            pl.when((g >= done) & (g < done + length))(functools.partial(run, ref, first))
        done += length


def run_chunk(spots, slot, rows, pieces, student, bias, target, cols, stats=(), kept=None, tokens=0, state=None):
    _, lanes = student.shape
    step = bias.shape[-1]
    lines = (rows // step,) + bias.shape[1:]
    spans = [(length, local is None) for _, length, local in pieces]
    moved = pl.BlockSpec((rows, lanes), lambda g, pref: (pref[3 * (slot + g)], 0))
    after = pl.BlockSpec(lines, lambda g, pref: (pref[3 * (slot + g)], 0, 0))

    def fixed(height):
        return pl.BlockSpec((height, lanes), lambda g, pref: (0, 0))

    in_specs, operands = [], [spots]
    done = 0
    for array, length, local in pieces:
        def where(g, pref, done=done, length=length, local=local):
            mine = jnp.clip(g - done, 0, length - 1)
            return ((pref[3 * (slot + done + mine)] if local else mine), 0)

        if local is None:
            in_specs.append(pl.BlockSpec(memory_space=pltpu.VMEM))
            array = pltpu.with_memory_space_constraint(array, pltpu.VMEM)
        else:
            in_specs.append(pl.BlockSpec((rows, lanes), where))
        operands.append(array)
        done += length
    in_specs += [moved, after, fixed(1)]
    operands += [student, bias, target]
    out_shape = [jax.ShapeDtypeStruct(student.shape, BF16)]
    out_specs = [moved]
    aliases = {}
    if stats:
        in_specs += [fixed(8)] * len(stats) + [fixed(1)]
        operands += list(stats) + [kept]
        out_shape += [jax.ShapeDtypeStruct((16, lanes), F32), jax.ShapeDtypeStruct((8, lanes), F32)]
        out_specs += [fixed(16), fixed(8)]
    else:
        vec, div, grad = state
        in_specs += [fixed(8), fixed(16), pl.BlockSpec(memory_space=pl.ANY)]
        operands += [vec, div, grad]
        aliases = {len(operands) - 1: 0}
        out_shape.append(jax.ShapeDtypeStruct((16, lanes), F32))
        out_specs.append(fixed(16))
    scratch = [pltpu.VMEM((LINES, 2 * lanes), BF16)]

    def kernel(*refs):
        chunk_kernel(*refs, spans=spans, slot=slot, step=step, cols=cols, shares=len(stats), tokens=tokens)

    return pl.pallas_call(
        kernel,
        out_shape=tuple(out_shape),
        grid_spec=pltpu.PrefetchScalarGridSpec(
            num_scalar_prefetch=1,
            grid=(sum(length for length, _ in spans),),
            in_specs=in_specs,
            out_specs=tuple(out_specs),
            scratch_shapes=scratch,
        ),
        input_output_aliases=aliases,
        compiler_params=pltpu.CompilerParams(dimension_semantics=("arbitrary",)),
        name="chunk",
    )(*operands)


def hits(base, r, tgt_ref, step, lanes, limit):
    gap = wide_rows(tgt_ref[...], 8) - lax.broadcasted_iota(jnp.int32, (8, lanes), 0) - (base + r)
    line = jnp.where((gap & 7) == 0, gap >> 3, -1)
    tile = lax.broadcasted_iota(jnp.int32, (step // 8, 8, lanes), 0)
    hit = (tile == line[None]).reshape(step, lanes)
    if limit is not None:
        hit = hit & (lax.broadcasted_iota(jnp.int32, (step, lanes), 0) < limit - r)
    return hit


def tail_sum_kernel(t_ref, s_ref, m_ref, vec_ref, tgt_ref, d_ref, o_ref, *, first_id, limit):
    rows, lanes = t_ref.shape
    step = m_ref.shape[-1]
    weights = addend_rows([vec_ref[0:1, :]], [1], 3)
    base = first_id()
    div = jnp.zeros((8, lanes), F32)
    picked = jnp.zeros((8, lanes), F32)
    for n in range(rows // step):
        t = t_ref[n * step:(n + 1) * step, :].astype(F32)
        s = s_ref[n * step:(n + 1) * step, :].astype(F32)
        tp = jnp.exp(t + addend(m_ref, n, weights))
        div = div + fold(jnp.sum, tp * (t - s))
        hit = hits(base, n * step, tgt_ref, step, lanes, limit)
        picked = picked + fold(jnp.sum, jnp.where(hit, s, 0.0))
    total = div - wide_rows(vec_ref[2:3, :], 8) * picked
    o_ref[...] = jnp.sum(total, axis=0, keepdims=True) + d_ref[...]


def tail_grad_kernel(t_ref, s_ref, m_ref, vec_ref, tgt_ref, _, g_ref, out, sems, *, first_id, first_row, limit):
    rows, lanes = t_ref.shape
    step = m_ref.shape[-1]
    weights = addend_rows([vec_ref[0:1, :], vec_ref[1:2, :]], [1, 1], 3)
    weight = wide_rows(vec_ref[2:3, :], step)
    base = first_id()
    row = first_row()
    copies = []
    for n in range(rows // step):
        part = pl.ds(n * step, step)
        both = addend(m_ref, n, weights)
        tp = jnp.exp(t_ref[part, :].astype(F32) + both[:, :lanes])
        sp = jnp.exp(s_ref[part, :].astype(F32) + both[:, lanes:])
        hit = hits(base, n * step, tgt_ref, step, lanes, limit)
        out[part, :] = ((sp - tp) - jnp.where(hit, weight, 0.0)).astype(BF16)
        place = pl.ds(pl.multiple_of(row + n * step, ROWS), step)
        copies.append(pltpu.make_async_copy(out.at[part, :], g_ref.at[place, :], sems.at[n]))
        copies[-1].start()
    for copy in copies:
        copy.wait()


def held(value):
    return pltpu.with_memory_space_constraint(value, pltpu.VMEM)


def run_tail_sum(operands, first_id, limit):
    lanes = operands[0].shape[1]

    def kernel(*refs):
        tail_sum_kernel(*refs, first_id=first_id, limit=limit)

    return pl.pallas_call(
        kernel,
        out_shape=pltpu.VMEM((1, lanes), F32),
        in_specs=[pl.BlockSpec(memory_space=pltpu.VMEM)] * len(operands),
        out_specs=pl.BlockSpec(memory_space=pltpu.VMEM),
        name="tail_sum",
    )(*[held(value) for value in operands])


def run_tail_grad(operands, grad, first_id, first_row, limit):
    rows, lanes = operands[0].shape
    step = operands[2].shape[-1]

    def kernel(*refs):
        tail_grad_kernel(*refs, first_id=first_id, first_row=first_row, limit=limit)

    return pl.pallas_call(
        kernel,
        out_shape=jax.ShapeDtypeStruct(grad.shape, grad.dtype),
        in_specs=[pl.BlockSpec(memory_space=pltpu.VMEM)] * len(operands) + [pl.BlockSpec(memory_space=pl.ANY)],
        out_specs=pl.BlockSpec(memory_space=pl.ANY),
        scratch_shapes=[pltpu.VMEM((rows, lanes), BF16), pltpu.SemaphoreType.DMA((rows // step,))],
        input_output_aliases={len(operands): 0},
        name="tail_grad",
    )(*[held(value) for value in operands], grad)


def cut_kernel(t_ref, *rest, parts, held, partner):
    outs, rest = rest[:len(parts)], rest[len(parts):]
    stops = outs if held else rest[:len(parts)]
    sems = rest[-1]
    reads, writes = [], []
    me = lax.axis_index("voc")
    for k, (shift, start, size) in enumerate(parts):
        block = partner(me, shift)
        reads.append(pltpu.make_async_copy(t_ref.at[block, pl.ds(start, size), :], stops[k], sems.at[k]))
        reads[-1].start()
    for k in range(len(parts)):
        reads[k].wait()
        if not held:
            writes.append(pltpu.make_async_copy(stops[k], outs[k], sems.at[len(parts) + k]))
            writes[-1].start()
    for copy in writes:
        copy.wait()


def cut(teacher, parts, held, partner):
    lanes = teacher.shape[-1]
    space = pltpu.VMEM if held else pl.ANY
    scratch = [] if held else [pltpu.VMEM((size, lanes), BF16) for _, _, size in parts]

    def kernel(*refs):
        cut_kernel(*refs, parts=parts, held=held, partner=partner)

    return pl.pallas_call(
        kernel,
        out_shape=tuple(
            pltpu.VMEM((size, lanes), BF16) if held else jax.ShapeDtypeStruct((size, lanes), BF16)
            for _, _, size in parts),
        in_specs=[pl.BlockSpec(memory_space=pl.ANY)],
        out_specs=tuple(pl.BlockSpec(memory_space=space) for _ in parts),
        scratch_shapes=scratch + [pltpu.SemaphoreType.DMA((2 * len(parts),))],
        name="cut",
    )(teacher)


def plan(padded, voc_count):
    shifts = list(range(voc_count - 1, 0, -1))
    far = shifts[:-1] if len(shifts) > 1 else shifts
    near = shifts[len(far):]
    big = largest_part(padded, 1600)
    small = largest_part(padded, 544)
    chunked = padded == 3 * big and big == 3 * small
    pieces = []
    for index, shift in enumerate(far):
        if chunked and index == 0:
            pieces += [(shift, 0, big, big), (shift, big, 2 * big, big)]
        elif chunked and index == len(far) - 1:
            pieces += [(shift, 0, 2 * big, big), (shift, 2 * big, big, big)]
        else:
            pieces.append((shift, 0, padded, big))
    late = [k for k, piece in enumerate(pieces) if len(far) > 1 and piece[0] == far[-1]]
    pieces += [(shift, 0, padded, big) for shift in near]
    early = [k for k in range(len(pieces)) if k not in late]
    return pieces, early, late, big


def body(teacher_logits, student_logits, target_ids, vocab_used):
    tok_rows, vocab_cols = teacher_logits.shape
    voc_count = lax.axis_size("voc")
    voc_index = lax.axis_index("voc")
    tok_count = lax.axis_size("tok")
    block_cols = vocab_cols // voc_count
    padded = -(-block_cols // ROWS) * ROWS
    split = padded != block_cols
    paired = voc_count & (voc_count - 1) == 0

    def partner(index, shift):
        return index ^ shift if paired else (index + shift) % voc_count

    def source(index, shift):
        return index ^ shift if paired else (index - shift) % voc_count

    def swap(value, shift):
        return lax.ppermute(value, "voc", [(i, partner(i, shift)) for i in range(voc_count)])

    def blocked(matrix):
        shaped = matrix.T.reshape(voc_count, block_cols, tok_rows)
        if split:
            shaped = jnp.pad(shaped, ((0, 0), (0, padded - block_cols), (0, 0)))
        return shaped

    teacher = blocked(teacher_logits)
    flat = teacher.reshape(voc_count * padded, tok_rows)
    student = blocked(student_logits).reshape(voc_count * padded, tok_rows)
    pieces, early, late, big = plan(padded, voc_count)

    cuts = [piece[:3] for piece in pieces]
    parts = list(cut(teacher, cuts[:1], True, partner))
    parts += list(cut(teacher, cuts[1:], False, partner))
    arrived = []
    for k, piece in enumerate(pieces):
        arrived.append(swap(parts[k], piece[0]))

    target = target_ids.reshape(1, tok_rows)
    kept = (target >= 0).astype(F32)
    if tok_count & (tok_count - 1):
        kept = lax.psum(kept, "tok")
    else:
        for step in range(tok_count.bit_length() - 1):
            pairs = [(i, i ^ 1 << step) for i in range(tok_count)]
            if step == 0:
                kept = kept + (lax.ppermute(target, "tok", pairs) >= 0).astype(F32)
            else:
                kept = kept + lax.ppermute(kept, "tok", pairs)

    flags = vocab_used.reshape(voc_count, voc_count, block_cols)
    flags = jnp.stack([
        lax.dynamic_index_in_dim(flags, voc_index, 0, keepdims=False),
        lax.dynamic_index_in_dim(flags, voc_index, 1, keepdims=False),
    ])
    line = jnp.where(flags == 1, 0.0, NEG).astype(BF16).reshape(2 * voc_count, block_cols)
    if split:
        line = jnp.pad(line, ((0, 0), (0, padded - block_cols)), constant_values=NEG)
    step = largest_part(padded, STEP)
    line = line.reshape(2, voc_count * padded // step, 1, step)
    kind = lax.broadcasted_iota(jnp.int32, (1, LINES, 1), 1)
    ones = jnp.where(kind < 5, 1.0, 0.0).astype(BF16)
    bias = jnp.where(kind == 0, line[0], jnp.where(kind == 1, line[1], ones))

    stats = run_stats(flat, student, bias, 1600)
    gathered = [stats]
    for shift in range(1, voc_count):
        gathered.append(swap(stats, shift))

    shift_of, scale, own, fixed = [], [], [], []

    def note(shift, start, size, rows):
        for at in range(start, start + size, rows):
            shift_of.extend([shift] * 3)
            scale.extend([padded // rows, voc_count * block_cols, 0])
            own.extend([0, block_cols, 0])
            fixed.extend([at // rows, at, at])
        return size // rows

    groups = []
    held = [pair[1] for pair in sorted((piece[2], k) for k, piece in enumerate(pieces))]
    held = late + [k for k in reversed(held) if k in early]
    size = 0
    for n, k in enumerate(held):
        size += pieces[k][2] * tok_rows * 2
        if size > HELD_BYTES:
            held = held[:n]
            break
    first = [(flat, note(0, 0, padded, big), True)]
    for k in sorted(early, key=lambda k: k < len(pieces) - 1):
        if pieces[k][3] == big:
            first.append((arrived[k], note(*pieces[k]), None if k in held else False))
    used = sum(length for _, length, _ in first)
    apart = [k for k in early if pieces[k][3] != big]
    for k in late:
        group = []
        start = used
        for j in apart + [k]:
            group.append((arrived[j], note(*pieces[j]), None if j in held else False))
            used += group[-1][1]
        groups.append((start, pieces[k][3], group))
        apart = []
    blocks = source(voc_index, np.array(shift_of, np.int32))
    spots = blocks * np.array(scale, np.int32) + voc_index * np.array(own, np.int32) + np.array(fixed, np.int32)
    spots = spots.astype(jnp.int32)

    cols = block_cols if split else None
    grad, div, vec = run_chunk(
        spots, 0, big, first, student, bias, target, cols, stats=gathered, kept=kept,
        tokens=tok_rows * tok_count)
    for slot, rows, piece in groups[:-1]:
        grad, div = run_chunk(spots, slot, rows, piece, student, bias, target, cols, state=(vec, div, grad))
    if groups:
        shift, start, size, _ = pieces[late[-1]]

        def first_row(me=None):
            return source(lax.axis_index("voc") if me is None else me, shift) * padded + start

        def first_id():
            me = lax.axis_index("voc")
            return (source(me, shift) * voc_count + me) * block_cols + start

        step = bias.shape[-1]
        row = first_row(voc_index)
        rows = lax.dynamic_slice(student, (row, 0), (size, tok_rows))
        lines = lax.dynamic_slice(bias, (row // step, 0, 0), (size // step,) + bias.shape[1:])
        operands = [arrived[late[-1]], rows, lines, vec, target]
        limit = block_cols - start if split else None
        div = jnp.sum(div[:8] - vec[2:3] * div[8:], axis=0, keepdims=True) + vec[3:4]
        div = run_tail_sum(operands + [div], first_id, limit)
        grad = run_tail_grad(operands, grad, first_id, first_row, limit)
    else:
        div = jnp.sum(div[:8] - vec[2:3] * div[8:], axis=0, keepdims=True) + vec[3:4]
    loss = div
    for shift in range(1, voc_count):
        loss = loss + swap(div, shift)
    gradient = grad.reshape(voc_count, padded, tok_rows)[:, :block_cols].reshape(vocab_cols, tok_rows).T
    return (gradient, loss.reshape(tok_rows))


def solution(mesh):
    placed = (P("tok", "voc"), P("tok", "voc"), P("tok"), P())

    step = jax.shard_map(body, mesh=mesh, in_specs=placed, out_specs=(P("tok", "voc"), P("tok")), check_vma=False)

    def whole(teacher_logits, student_logits, target_ids, vocab_used):
        run = step
        return run(teacher_logits, student_logits, target_ids, vocab_used)

    return whole
```

```python
import functools

import jax
import jax.numpy as jnp
import numpy as np
from jax import lax
from jax.experimental import pallas as pl
from jax.experimental.pallas import tpu as pltpu
from jax.sharding import PartitionSpec as P

NEG = -1e30
LOW = -3e38
ROWS = 16
LINES = 8
SPLITS = 3
HELD_BYTES = 2.4 * 2**20
WAYS = 3
STEP = 544
LN2 = 0.6931471805599453
F32 = jnp.float32
BF16 = jnp.bfloat16


def largest_part(total, limit):
    best = ROWS
    for size in range(ROWS, limit + 1, ROWS):
        if total % size == 0:
            best = size
    return best


def fold(op, value, height=8):
    return op(value.reshape(-1, height, value.shape[-1]), axis=0)


def addend_rows(rows, masks, pieces):
    parts = []
    for row, mask in zip(rows, masks):
        left = -row
        part = [jnp.ones_like(row) if k == mask else jnp.zeros_like(row) for k in range(2)]
        for _ in range(pieces):
            piece = left.astype(BF16).astype(F32)
            part.append(piece)
            left = left - piece
        part.append(jnp.zeros((LINES - 2 - pieces, row.shape[1]), F32))
        parts.append(jnp.concatenate(part, axis=0))
    return jnp.concatenate(parts, axis=1).astype(BF16)


def addend(mask_ref, n, weights):
    return lax.dot_general(mask_ref[n], weights, (((0,), (0,)), ((), ())), preferred_element_type=F32)


def wide_rows(line, height):
    return jnp.broadcast_to(line, (height, line.shape[-1]))


def stats_kernel(t_ref, s_ref, m_ref, o_ref, tops, sums, block, *, step):
    g = pl.program_id(0)
    rows, lanes = t_ref.shape
    steps = rows // step
    tiles = step // ROWS

    @pl.when(g == 0)
    def _():
        tops[...] = jnp.full(tops.shape, LOW, F32)
        sums[...] = jnp.zeros(sums.shape, F32)

    def part(n):
        return pl.ds(pl.multiple_of(n * step, step), step)

    def first(n, carry):
        tops = list(carry)
        for k in range(tiles):
            tile = pl.ds(pl.multiple_of(n * step + k * ROWS, ROWS), ROWS)
            at = k % WAYS
            tops[at] = jnp.maximum(tops[at], t_ref[tile, :].astype(F32))
            tops[WAYS + at] = jnp.maximum(tops[WAYS + at], s_ref[tile, :].astype(F32))
        return tuple(tops)

    low = jnp.full((ROWS, lanes), LOW, F32)
    highs = lax.fori_loop(0, steps, first, (low,) * (2 * WAYS), unroll=True)
    t_top, s_top = [
        jnp.max(functools.reduce(jnp.maximum, highs[k:k + WAYS]), axis=0, keepdims=True)
        for k in (0, WAYS)]
    weights = addend_rows([t_top, s_top], [0, 1], 1)

    def second(n, carry):
        both = addend(m_ref, n, weights)
        t = t_ref[part(n), :].astype(F32) + both[:, :lanes]
        s = s_ref[part(n), :].astype(F32) + both[:, lanes:]
        return (carry[0] + fold(jnp.sum, jnp.exp(t)), carry[1] + fold(jnp.sum, jnp.exp(s)))

    zero = jnp.zeros((8, lanes), F32)
    t_sum, s_sum = [
        jnp.sum(total, axis=0, keepdims=True)
        for total in lax.fori_loop(0, steps, second, (zero, zero), unroll=True)]
    block[0:1, :] = t_top
    block[1:2, :] = t_sum
    block[2:3, :] = s_top
    block[3:4, :] = s_sum

    @pl.when(jnp.min(jnp.minimum(t_sum, s_sum)) < 1e-10)
    def _():
        blank = jnp.zeros((1, lanes), F32)
        plain = addend_rows([blank, blank], [0, 1], 1)

        def masked(n):
            both = addend(m_ref, n, plain)
            return (
                t_ref[part(n), :].astype(F32) + both[:, :lanes],
                s_ref[part(n), :].astype(F32) + both[:, lanes:])

        def high(n, carry):
            return tuple(jnp.maximum(top, fold(jnp.max, value)) for top, value in zip(carry, masked(n)))

        low = jnp.full((8, lanes), LOW, F32)
        tops = [jnp.max(top, axis=0, keepdims=True) for top in lax.fori_loop(0, steps, high, (low, low))]

        def gather(n, carry):
            return tuple(
                total + fold(jnp.sum, jnp.exp(value - wide_rows(top, step)))
                for total, value, top in zip(carry, masked(n), tops))

        totals = lax.fori_loop(0, steps, gather, (zero, zero))
        for k in range(2):
            block[2 * k:2 * k + 1, :] = tops[k]
            block[2 * k + 1:2 * k + 2, :] = jnp.sum(totals[k], axis=0, keepdims=True)

    for k in range(2):
        old = tops[k:k + 1, :]
        top = block[2 * k:2 * k + 1, :]
        new = jnp.maximum(old, top)
        sums[k:k + 1, :] = (
            sums[k:k + 1, :] * jnp.exp(old - new) + block[2 * k + 1:2 * k + 2, :] * jnp.exp(top - new))
        tops[k:k + 1, :] = new

    @pl.when(g == pl.num_programs(0) - 1)
    def _():
        o_ref[...] = jnp.concatenate(
            [tops[0:1, :], sums[0:1, :], tops[1:2, :], sums[1:2, :], jnp.zeros((4, lanes), F32)], axis=0)


def run_stats(teacher, student, mask, limit):
    total, lanes = teacher.shape
    rows = largest_part(total, limit)
    count = total // rows
    near = pl.BlockSpec((rows, lanes), lambda g: (g, 0))
    step = mask.shape[-1]
    lines = (rows // step,) + mask.shape[1:]
    held = pl.BlockSpec(lines, lambda g: (g, 0, 0))

    def kernel(*refs):
        stats_kernel(*refs, step=step)

    return pl.pallas_call(
        kernel,
        out_shape=jax.ShapeDtypeStruct((8, lanes), F32),
        grid=(count,),
        in_specs=[near, near, held],
        out_specs=pl.BlockSpec((8, lanes), lambda g: (0, 0)),
        scratch_shapes=[pltpu.VMEM((8, lanes), F32)] * 3,
        compiler_params=pltpu.CompilerParams(dimension_semantics=("arbitrary",)),
        name="stats",
    )(teacher, student, mask)


def join_stats(refs, kept, target, tokens):
    parts = [ref[...] for ref in refs]
    t_top = parts[0][0:1]
    s_top = parts[0][2:3]
    for part in parts[1:]:
        t_top = jnp.maximum(t_top, part[0:1])
        s_top = jnp.maximum(s_top, part[2:3])
    t_sum = jnp.zeros_like(t_top)
    s_sum = jnp.zeros_like(t_top)
    for part in parts:
        t_sum = t_sum + part[1:2] * jnp.exp(part[0:1] - t_top)
        s_sum = s_sum + part[3:4] * jnp.exp(part[2:3] - s_top)
    t_lse = t_top + jnp.log(t_sum)
    s_lse = s_top + jnp.log(s_sum)
    count = jnp.sum(kept, axis=1, keepdims=True)
    weight = jnp.where(target >= 0, (0.5 * tokens) / count, 0.0)
    base = (0.5 * (s_lse - t_lse) + weight * s_lse) * (1.0 / len(parts))
    blank = jnp.zeros((4, target.shape[1]), F32)
    return jnp.concatenate([t_lse + LN2, s_lse - jnp.log(0.5 + weight), weight, base, blank], axis=0)


def chunk_kernel(spots, *refs, spans, slot, step, cols, shares, tokens):
    pieces, refs = refs[:len(spans)], refs[len(spans):]
    s_ref, b_ref, tgt_ref = refs[:3]
    refs = refs[3:]
    g = pl.program_id(0)
    rows, lanes = s_ref.shape
    weights_ref, refs = refs[-1], refs[:-1]
    if shares:
        share_refs, (kept_ref, g_ref, d_out, vec_ref) = refs[:shares], refs[shares:]

        @pl.when(g == 0)
        def _():
            vec_ref[...] = join_stats(share_refs, kept_ref[...], tgt_ref[...], tokens)
            d_out[...] = jnp.zeros(d_out.shape, F32)
    else:
        vec_ref, d_in, _, g_ref, d_out = refs

        @pl.when(g == 0)
        def _():
            d_out[...] = d_in[...]

    @pl.when(g == 0)
    def _():
        weights_ref[...] = addend_rows([vec_ref[0:1, :], vec_ref[1:2, :]], [1, 1], 3)

    at = 3 * (slot + g)
    base = spots[at + 1]
    away = wide_rows(tgt_ref[...], 8) - lax.broadcasted_iota(jnp.int32, (8, lanes), 0)
    tile = lax.broadcasted_iota(jnp.int32, (step // 8, 8, lanes), 0)
    weight = wide_rows(vec_ref[2:3, :], step)
    weights = weights_ref[...]

    def run(t_ref, first=0):
        def body(n, carry):
            div, picked = carry
            r = pl.multiple_of(n * step, step)
            both = addend(b_ref, n, weights)
            t = t_ref[pl.ds(first + r, step), :].astype(F32)
            s = s_ref[pl.ds(r, step), :].astype(F32)
            tp = jnp.exp(t + both[:, :lanes])
            sp = jnp.exp(s + both[:, lanes:])
            gap = away - (base + r)
            line = jnp.where((gap & 7) == 0, gap >> 3, -1)
            hit = (tile == line[None]).reshape(step, lanes)
            if cols is not None:
                hit = hit & (lax.broadcasted_iota(jnp.int32, (step, lanes), 0) + (spots[at + 2] + r) < cols)
            grad = (sp - tp) - jnp.where(hit, weight, 0.0)
            g_ref[pl.ds(r, step), :] = grad.astype(BF16)
            div = div + fold(jnp.sum, tp * (t - s))
            picked = picked + fold(jnp.sum, jnp.where(hit, s, 0.0))
            return (div, picked)

        div, picked = lax.fori_loop(0, rows // step, body, (d_out[0:8, :], d_out[8:16, :]), unroll=True)
        d_out[0:8, :] = div
        d_out[8:16, :] = picked

    done = 0
    for ref, (length, held) in zip(pieces, spans):
        first = pl.multiple_of((g - done) * rows, rows) if held else 0
        if len(pieces) == 1:
            run(ref, first)
        else:
            pl.when((g >= done) & (g < done + length))(functools.partial(run, ref, first))
        done += length


def run_chunk(spots, slot, rows, pieces, student, bias, target, cols, stats=(), kept=None, tokens=0, state=None):
    _, lanes = student.shape
    step = bias.shape[-1]
    lines = (rows // step,) + bias.shape[1:]
    spans = [(length, local is None) for _, length, local in pieces]
    moved = pl.BlockSpec((rows, lanes), lambda g, pref: (pref[3 * (slot + g)], 0))
    after = pl.BlockSpec(lines, lambda g, pref: (pref[3 * (slot + g)], 0, 0))

    def fixed(height):
        return pl.BlockSpec((height, lanes), lambda g, pref: (0, 0))

    in_specs, operands = [], [spots]
    done = 0
    for array, length, local in pieces:
        def where(g, pref, done=done, length=length, local=local):
            mine = jnp.clip(g - done, 0, length - 1)
            return ((pref[3 * (slot + done + mine)] if local else mine), 0)

        if local is None:
            in_specs.append(pl.BlockSpec(memory_space=pltpu.VMEM))
            array = pltpu.with_memory_space_constraint(array, pltpu.VMEM)
        else:
            in_specs.append(pl.BlockSpec((rows, lanes), where))
        operands.append(array)
        done += length
    in_specs += [moved, after, fixed(1)]
    operands += [student, bias, target]
    out_shape = [jax.ShapeDtypeStruct(student.shape, BF16)]
    out_specs = [moved]
    aliases = {}
    if stats:
        in_specs += [fixed(8)] * len(stats) + [fixed(1)]
        operands += list(stats) + [kept]
        out_shape += [jax.ShapeDtypeStruct((16, lanes), F32), jax.ShapeDtypeStruct((8, lanes), F32)]
        out_specs += [fixed(16), fixed(8)]
    else:
        vec, div, grad = state
        in_specs += [fixed(8), fixed(16), pl.BlockSpec(memory_space=pl.ANY)]
        operands += [vec, div, grad]
        aliases = {len(operands) - 1: 0}
        out_shape.append(jax.ShapeDtypeStruct((16, lanes), F32))
        out_specs.append(fixed(16))
    scratch = [pltpu.VMEM((LINES, 2 * lanes), BF16)]

    def kernel(*refs):
        chunk_kernel(*refs, spans=spans, slot=slot, step=step, cols=cols, shares=len(stats), tokens=tokens)

    return pl.pallas_call(
        kernel,
        out_shape=tuple(out_shape),
        grid_spec=pltpu.PrefetchScalarGridSpec(
            num_scalar_prefetch=1,
            grid=(sum(length for length, _ in spans),),
            in_specs=in_specs,
            out_specs=tuple(out_specs),
            scratch_shapes=scratch,
        ),
        input_output_aliases=aliases,
        compiler_params=pltpu.CompilerParams(dimension_semantics=("arbitrary",)),
        name="chunk",
    )(*operands)


def hits(base, r, tgt_ref, step, lanes, limit):
    gap = wide_rows(tgt_ref[...], 8) - lax.broadcasted_iota(jnp.int32, (8, lanes), 0) - (base + r)
    line = jnp.where((gap & 7) == 0, gap >> 3, -1)
    tile = lax.broadcasted_iota(jnp.int32, (step // 8, 8, lanes), 0)
    hit = (tile == line[None]).reshape(step, lanes)
    if limit is not None:
        hit = hit & (lax.broadcasted_iota(jnp.int32, (step, lanes), 0) < limit - r)
    return hit


def tail_sum_kernel(t_ref, s_ref, m_ref, vec_ref, tgt_ref, d_ref, o_ref, *, first_id, limit):
    rows, lanes = t_ref.shape
    step = m_ref.shape[-1]
    weights = addend_rows([vec_ref[0:1, :]], [1], 3)
    base = first_id()
    div = jnp.zeros((8, lanes), F32)
    picked = jnp.zeros((8, lanes), F32)
    for n in range(rows // step):
        t = t_ref[n * step:(n + 1) * step, :].astype(F32)
        s = s_ref[n * step:(n + 1) * step, :].astype(F32)
        tp = jnp.exp(t + addend(m_ref, n, weights))
        div = div + fold(jnp.sum, tp * (t - s))
        hit = hits(base, n * step, tgt_ref, step, lanes, limit)
        picked = picked + fold(jnp.sum, jnp.where(hit, s, 0.0))
    total = div - wide_rows(vec_ref[2:3, :], 8) * picked
    o_ref[...] = jnp.sum(total, axis=0, keepdims=True) + d_ref[...]


def tail_grad_kernel(t_ref, s_ref, m_ref, vec_ref, tgt_ref, _, g_ref, out, sems, *, first_id, first_row, limit):
    rows, lanes = t_ref.shape
    step = m_ref.shape[-1]
    weights = addend_rows([vec_ref[0:1, :], vec_ref[1:2, :]], [1, 1], 3)
    weight = wide_rows(vec_ref[2:3, :], step)
    base = first_id()
    row = first_row()
    copies = []
    for n in range(rows // step):
        part = pl.ds(n * step, step)
        both = addend(m_ref, n, weights)
        tp = jnp.exp(t_ref[part, :].astype(F32) + both[:, :lanes])
        sp = jnp.exp(s_ref[part, :].astype(F32) + both[:, lanes:])
        hit = hits(base, n * step, tgt_ref, step, lanes, limit)
        out[part, :] = ((sp - tp) - jnp.where(hit, weight, 0.0)).astype(BF16)
        place = pl.ds(pl.multiple_of(row + n * step, ROWS), step)
        copies.append(pltpu.make_async_copy(out.at[part, :], g_ref.at[place, :], sems.at[n]))
        copies[-1].start()
    for copy in copies:
        copy.wait()


def held(value):
    return pltpu.with_memory_space_constraint(value, pltpu.VMEM)


def run_tail_sum(operands, first_id, limit):
    lanes = operands[0].shape[1]

    def kernel(*refs):
        tail_sum_kernel(*refs, first_id=first_id, limit=limit)

    return pl.pallas_call(
        kernel,
        out_shape=pltpu.VMEM((1, lanes), F32),
        in_specs=[pl.BlockSpec(memory_space=pltpu.VMEM)] * len(operands),
        out_specs=pl.BlockSpec(memory_space=pltpu.VMEM),
        name="tail_sum",
    )(*[held(value) for value in operands])


def run_tail_grad(operands, grad, first_id, first_row, limit):
    rows, lanes = operands[0].shape
    step = operands[2].shape[-1]

    def kernel(*refs):
        tail_grad_kernel(*refs, first_id=first_id, first_row=first_row, limit=limit)

    return pl.pallas_call(
        kernel,
        out_shape=jax.ShapeDtypeStruct(grad.shape, grad.dtype),
        in_specs=[pl.BlockSpec(memory_space=pltpu.VMEM)] * len(operands) + [pl.BlockSpec(memory_space=pl.ANY)],
        out_specs=pl.BlockSpec(memory_space=pl.ANY),
        scratch_shapes=[pltpu.VMEM((rows, lanes), BF16), pltpu.SemaphoreType.DMA((rows // step,))],
        input_output_aliases={len(operands): 0},
        name="tail_grad",
    )(*[held(value) for value in operands], grad)


def cut_kernel(t_ref, *rest, parts, held, partner):
    outs, rest = rest[:len(parts)], rest[len(parts):]
    stops = outs if held else rest[:len(parts)]
    sems = rest[-1]
    reads, writes = [], []
    me = lax.axis_index("voc")
    for k, (shift, start, size) in enumerate(parts):
        block = partner(me, shift)
        span = size // SPLITS if held and size % (SPLITS * ROWS) == 0 else size
        group = []
        for n in range(size // span):
            source = t_ref.at[block, pl.ds(start + n * span, span), :]
            group.append(pltpu.make_async_copy(source, stops[k].at[pl.ds(n * span, span), :], sems.at[k * SPLITS + n]))
            group[-1].start()
        reads.append(group)
    for k, group in enumerate(reads):
        for copy in group:
            copy.wait()
        if not held:
            writes.append(pltpu.make_async_copy(stops[k], outs[k], sems.at[len(parts) * SPLITS + k]))
            writes[-1].start()
    for copy in writes:
        copy.wait()


def cut(teacher, parts, held, partner):
    lanes = teacher.shape[-1]
    space = pltpu.VMEM if held else pl.ANY
    scratch = [] if held else [pltpu.VMEM((size, lanes), BF16) for _, _, size in parts]

    def kernel(*refs):
        cut_kernel(*refs, parts=parts, held=held, partner=partner)

    return pl.pallas_call(
        kernel,
        out_shape=tuple(
            pltpu.VMEM((size, lanes), BF16) if held else jax.ShapeDtypeStruct((size, lanes), BF16)
            for _, _, size in parts),
        in_specs=[pl.BlockSpec(memory_space=pl.ANY)],
        out_specs=tuple(pl.BlockSpec(memory_space=space) for _ in parts),
        scratch_shapes=scratch + [pltpu.SemaphoreType.DMA((len(parts) * (SPLITS + 1),))],
        name="cut",
    )(teacher)


def plan(padded, voc_count):
    shifts = list(range(voc_count - 1, 0, -1))
    far = shifts[:-1] if len(shifts) > 1 else shifts
    near = shifts[len(far):]
    big = largest_part(padded, 1600)
    small = largest_part(padded, 544)
    chunked = padded == 3 * big and big == 3 * small
    pieces = []
    for index, shift in enumerate(far):
        if chunked and index == 0:
            pieces += [(shift, 0, big, big), (shift, big, 2 * big, big)]
        elif chunked and index == len(far) - 1:
            pieces += [(shift, 0, 2 * big, big), (shift, 2 * big, big, big)]
        else:
            pieces.append((shift, 0, padded, big))
    late = [k for k, piece in enumerate(pieces) if len(far) > 1 and piece[0] == far[-1]]
    pieces += [(shift, 0, padded, big) for shift in near]
    early = [k for k in range(len(pieces)) if k not in late]
    return pieces, early, late, big


def body(teacher_logits, student_logits, target_ids, vocab_used):
    tok_rows, vocab_cols = teacher_logits.shape
    voc_count = lax.axis_size("voc")
    voc_index = lax.axis_index("voc")
    tok_count = lax.axis_size("tok")
    block_cols = vocab_cols // voc_count
    padded = -(-block_cols // ROWS) * ROWS
    split = padded != block_cols
    paired = voc_count & (voc_count - 1) == 0

    def partner(index, shift):
        return index ^ shift if paired else (index + shift) % voc_count

    def source(index, shift):
        return index ^ shift if paired else (index - shift) % voc_count

    def swap(value, shift):
        return lax.ppermute(value, "voc", [(i, partner(i, shift)) for i in range(voc_count)])

    def blocked(matrix):
        shaped = matrix.T.reshape(voc_count, block_cols, tok_rows)
        if split:
            shaped = jnp.pad(shaped, ((0, 0), (0, padded - block_cols), (0, 0)))
        return shaped

    teacher = blocked(teacher_logits)
    flat = teacher.reshape(voc_count * padded, tok_rows)
    student = blocked(student_logits).reshape(voc_count * padded, tok_rows)
    pieces, early, late, big = plan(padded, voc_count)

    cuts = [piece[:3] for piece in pieces]
    parts = list(cut(teacher, cuts[:1], True, partner))
    parts += list(cut(teacher, cuts[1:], False, partner))
    arrived = []
    for k, piece in enumerate(pieces):
        arrived.append(swap(parts[k], piece[0]))

    target = target_ids.reshape(1, tok_rows)
    kept = (target >= 0).astype(F32)
    if tok_count & (tok_count - 1):
        kept = lax.psum(kept, "tok")
    else:
        for step in range(tok_count.bit_length() - 1):
            pairs = [(i, i ^ 1 << step) for i in range(tok_count)]
            if step == 0:
                kept = kept + (lax.ppermute(target, "tok", pairs) >= 0).astype(F32)
            else:
                kept = kept + lax.ppermute(kept, "tok", pairs)

    flags = vocab_used.reshape(voc_count, voc_count, block_cols)
    flags = jnp.stack([
        lax.dynamic_index_in_dim(flags, voc_index, 0, keepdims=False),
        lax.dynamic_index_in_dim(flags, voc_index, 1, keepdims=False),
    ])
    line = jnp.where(flags == 1, 0.0, NEG).astype(BF16).reshape(2 * voc_count, block_cols)
    if split:
        line = jnp.pad(line, ((0, 0), (0, padded - block_cols)), constant_values=NEG)
    step = largest_part(padded, STEP)
    line = line.reshape(2, voc_count * padded // step, 1, step)
    kind = lax.broadcasted_iota(jnp.int32, (1, LINES, 1), 1)
    ones = jnp.where(kind < 5, 1.0, 0.0).astype(BF16)
    bias = jnp.where(kind == 0, line[0], jnp.where(kind == 1, line[1], ones))

    stats = run_stats(flat, student, bias, 1600)
    gathered = [stats]
    for shift in range(1, voc_count):
        gathered.append(swap(stats, shift))

    shift_of, scale, own, fixed = [], [], [], []

    def note(shift, start, size, rows):
        for at in range(start, start + size, rows):
            shift_of.extend([shift] * 3)
            scale.extend([padded // rows, voc_count * block_cols, 0])
            own.extend([0, block_cols, 0])
            fixed.extend([at // rows, at, at])
        return size // rows

    groups = []
    held = [pair[1] for pair in sorted((piece[2], k) for k, piece in enumerate(pieces))]
    held = late + [k for k in reversed(held) if k in early]
    size = 0
    for n, k in enumerate(held):
        size += pieces[k][2] * tok_rows * 2
        if size > HELD_BYTES:
            held = held[:n]
            break
    first = [(flat, note(0, 0, padded, big), True)]
    for k in sorted(early, key=lambda k: k < len(pieces) - 1):
        if pieces[k][3] == big:
            first.append((arrived[k], note(*pieces[k]), None if k in held else False))
    used = sum(length for _, length, _ in first)
    apart = [k for k in early if pieces[k][3] != big]
    for k in late:
        group = []
        start = used
        for j in apart + [k]:
            group.append((arrived[j], note(*pieces[j]), None if j in held else False))
            used += group[-1][1]
        groups.append((start, pieces[k][3], group))
        apart = []
    blocks = source(voc_index, np.array(shift_of, np.int32))
    spots = blocks * np.array(scale, np.int32) + voc_index * np.array(own, np.int32) + np.array(fixed, np.int32)
    spots = spots.astype(jnp.int32)

    cols = block_cols if split else None
    grad, div, vec = run_chunk(
        spots, 0, big, first, student, bias, target, cols, stats=gathered, kept=kept,
        tokens=tok_rows * tok_count)
    for slot, rows, piece in groups[:-1]:
        grad, div = run_chunk(spots, slot, rows, piece, student, bias, target, cols, state=(vec, div, grad))
    if groups:
        shift, start, size, _ = pieces[late[-1]]

        def first_row(me=None):
            return source(lax.axis_index("voc") if me is None else me, shift) * padded + start

        def first_id():
            me = lax.axis_index("voc")
            return (source(me, shift) * voc_count + me) * block_cols + start

        step = bias.shape[-1]
        row = first_row(voc_index)
        rows = lax.dynamic_slice(student, (row, 0), (size, tok_rows))
        lines = lax.dynamic_slice(bias, (row // step, 0, 0), (size // step,) + bias.shape[1:])
        operands = [arrived[late[-1]], rows, lines, vec, target]
        limit = block_cols - start if split else None
        div = jnp.sum(div[:8] - vec[2:3] * div[8:], axis=0, keepdims=True) + vec[3:4]
        div = run_tail_sum(operands + [div], first_id, limit)
        grad = run_tail_grad(operands, grad, first_id, first_row, limit)
    else:
        div = jnp.sum(div[:8] - vec[2:3] * div[8:], axis=0, keepdims=True) + vec[3:4]
    loss = div
    for shift in range(1, voc_count):
        loss = loss + swap(div, shift)
    gradient = grad.reshape(voc_count, padded, tok_rows)[:, :block_cols].reshape(vocab_cols, tok_rows).T
    return (gradient, loss.reshape(tok_rows))


def solution(mesh):
    placed = (P("tok", "voc"), P("tok", "voc"), P("tok"), P())

    step = jax.shard_map(body, mesh=mesh, in_specs=placed, out_specs=(P("tok", "voc"), P("tok")), check_vma=False)

    def whole(teacher_logits, student_logits, target_ids, vocab_used):
        run = step
        return run(teacher_logits, student_logits, target_ids, vocab_used)

    return whole
```
